32 devices in a mesh: chan: 4 (over y, x), tm: 8 (over z, core).
Axes of the slice: x: 2, y: 2, z: 4, core: 2. Of those that a mesh axis runs over, the one named last changes fastest.
Arguments:
- samples: bfloat16 [16, 2048, 1024], P('tm', 'chan'), may hold values from -6 to 6
- valid: int32 [16, 4], P('tm'), may hold values from 0 to 1, as said below
- plan: int32 [3, 4], replicated, may hold values from 0 to 3, as said below
Outputs:
- correlations: float32 [2048, 3, 129], P(('chan', 'tm'))
The draws below stay inside these ranges and needn't reach their ends.
Inputs may be any that keep to these rules, and one draw needn't show every extreme that they name: In each round every block is paired with another block and that block with it: plan[r, plan[r, b]] = b and plan[r, b] != b; no block meets the same partner in two rounds. valid[15, b] = 1 for every block b.
All inputs are finite; a program needn't handle non-finite values.
Results may differ from the reference program's by a relative error of at most 0.0053.
Values may be sent and summed in bfloat16 or wider, within the bound.
No kernel may reach another device: no remote copies, remote signals or barrier semaphores. Data moves between devices by JAX's collectives and lax.ppermute only.
A program may use at most 64 MiB of HBM per device.

```python
import math
import jax
import jax.numpy as jnp
from jax import lax

CHANNELS = 2048
LENGTH = 1024
BINS = 512
MAXLAG = 64
ROUNDS = 3
W = 16
BLOCKS = 4
BCH = 512


def draw_valid(key, part):
    rolled = jax.random.randint(key, (W, BLOCKS), 0, 100)
    window_idx = jnp.arange(W, dtype=jnp.int32)[:, None]
    keeping = rolled < 30 + 60 * window_idx // W
    keeping = keeping | (window_idx == W - 1)
    return keeping.astype(jnp.int32)


def draw_plan(key, part):
    key_perm = jax.random.fold_in(key, 11)
    key_start = jax.random.fold_in(key, 23)
    labels = jax.random.permutation(key_perm, BLOCKS).astype(jnp.int32)
    circle = jnp.argsort(labels, stable=True).astype(jnp.int32)
    first_turn = jax.random.randint(key_start, (), 0, BLOCKS - 1)
    modulus = BLOCKS - 1
    rows = []
    for step in range(ROUNDS):
        turn = (first_turn + step) % modulus
        mate = jnp.where(circle == modulus, turn, jnp.where(circle == turn, modulus, (2 * turn - circle) % modulus))
        rows.append(labels[mate])
    return jnp.stack(rows).astype(jnp.int32)


def block_scale(stream_key, dims, split, smallest, high):
    level, own = 1.0, jax.random.fold_in(stream_key, 6)
    for dim, shards_of in split:
        draws = jnp.exp(jax.random.uniform(jax.random.fold_in(own, dim), (shards_of,), jnp.float32, smallest / len(split), high / len(split)))
        level = level * jnp.repeat(draws, dims[dim] // shards_of).reshape([-1 if axis == dim else 1 for axis in range(len(dims))])
    return level


def scatter_about(stream_key, shape, width, most, pieces=(), kind=jnp.bfloat16):
    values = jax.random.normal(stream_key, shape, jnp.float32) * width
    if len(pieces) > 0:
        values = block_scale(stream_key, shape, pieces, -0.22, 0.18) * values
    return jnp.clip(values, min=-most, max=most).astype(kind)


def setup_inputs(seed: int = 0) -> dict:
    key_of = jax.random.split(jax.random.key(seed), 4)
    samples = scatter_about(key_of[0], (W, CHANNELS, LENGTH), 1.0, 6.0, ((0, 8), (1, 4)))
    valid = draw_valid(jax.random.fold_in(key_of[3], 71), 0)
    plan = draw_plan(jax.random.fold_in(key_of[3], 71), 0)
    return {"samples": samples, "valid": valid, "plan": plan}


def dft_table(length, count):
    sample_idx = jnp.arange(length, dtype=jnp.int32)[:, None]
    bin_idx = jnp.arange(count, dtype=jnp.int32)[None, :]
    phase = (sample_idx * bin_idx % length).astype(jnp.float32) * (2.0 * math.pi / length)
    return jnp.concatenate([jnp.cos(phase), -jnp.sin(phase)], axis=1).astype(jnp.bfloat16)

def lag_table(first_bin, count, length, maxlag):
    bin_idx = (first_bin + jnp.arange(count, dtype=jnp.int32))[:, None]
    shifts = jnp.arange(-maxlag, maxlag + 1, dtype=jnp.int32)[None, :]
    phase = (bin_idx * shifts % length).astype(jnp.float32) * (2.0 * math.pi / length)
    return jnp.concatenate([0.25 * jnp.cos(phase), -0.25 * jnp.sin(phase)], axis=0)

def reference(samples, valid, plan):
    table = dft_table(LENGTH, BINS)

    def whiten_one(window):
        spec = jnp.dot(window, table, preferred_element_type=jnp.float32).reshape(CHANNELS, 2, BINS)
        power = spec[:, 0] * spec[:, 0] + spec[:, 1] * spec[:, 1]
        level = lax.optimization_barrier(jnp.mean(power, axis=1, keepdims=True))
        white = spec / jnp.sqrt(power + 0.1 * level + 1e-06)[:, None, :]
        return white.astype(jnp.bfloat16)
    white = lax.map(whiten_one, samples)
    blocks = white.reshape(W, BLOCKS, BCH, 2, BINS)
    mask = valid.astype(jnp.float32)
    lags = lag_table(0, BINS, LENGTH, MAXLAG)
    results = []
    for step in range(ROUNDS):
        partner = plan[step]
        weight = mask * jnp.take(mask, partner, axis=1)
        count = lax.optimization_barrier(jnp.sum(weight, axis=0))

        def add(carry, item):
            own, wt = item
            other = jnp.take(own, partner, axis=0)
            first = own.astype(jnp.float32)
            second = other.astype(jnp.float32)
            real_part = first[:, :, 0] * second[:, :, 0] + first[:, :, 1] * second[:, :, 1]
            imag_part = first[:, :, 1] * second[:, :, 0] - first[:, :, 0] * second[:, :, 1]
            term = jnp.stack([real_part, imag_part], axis=2)
            return (carry + wt[:, None, None, None] * term, None)
        start = jnp.zeros((BLOCKS, BCH, 2, BINS), jnp.float32)
        stack, _ = lax.scan(add, start, (blocks, weight))
        stack = stack / count[:, None, None, None]
        corr = jnp.dot(stack.reshape(CHANNELS, 2 * BINS), lags, precision=lax.Precision.HIGHEST)
        results.append(corr)
    return jnp.stack(results, axis=1)
```

```python
import functools
import math

import jax
import jax.numpy as jnp
import numpy as np
from jax import lax
from jax.experimental import pallas as pl
from jax.experimental.pallas import tpu as pltpu
from jax.sharding import PartitionSpec as P

LAGS = 129
LANES = 128


def dft_table(length, count):
    sample_idx = np.arange(length, dtype=np.int64)[:, None]
    bin_idx = np.arange(count, dtype=np.int64)[None, :]
    phase = (sample_idx * bin_idx % length).astype(np.float64) * (2.0 * math.pi / length)
    return np.concatenate([np.cos(phase), -np.sin(phase)], axis=1)


def lag_table(count, length, shifts, sign):
    bin_idx = np.arange(count, dtype=np.int64)[:, None]
    phase = (bin_idx * shifts[None, :] % length).astype(np.float64) * (2.0 * math.pi / length)
    return np.concatenate([0.25 * np.cos(phase), -0.25 * sign * np.sin(phase)], axis=0)


def high_low(table):
    high = jnp.asarray(table.astype(np.float32)).astype(jnp.bfloat16)
    low = (jnp.asarray(table.astype(np.float32)) - high.astype(jnp.float32)).astype(jnp.bfloat16)
    return high, low


def split(value):
    high = value.astype(jnp.bfloat16)
    return high, (value - high.astype(jnp.float32)).astype(jnp.bfloat16)


def whiten(pieces, table, white):
    for slot, piece in enumerate(pieces):
        windows, rows, length = piece.shape
        bins = length // 2
        for window in range(windows):
            spec = jnp.dot(piece[window], table[...], preferred_element_type=jnp.float32)
            real, imag = spec[:, :bins], spec[:, bins:]
            power = real * real + imag * imag
            level = jnp.mean(power, axis=1, keepdims=True)
            scale = lax.rsqrt(power + 0.1 * level + 1e-06)
            white[slot, window, :, :bins] = (real * scale).astype(jnp.bfloat16)
            white[slot, window, :, bins:] = (imag * scale).astype(jnp.bfloat16)


def cross(white, first, second, row, rows):
    bins = white.shape[3] // 2
    real_sum, imag_sum = None, None
    for window in range(white.shape[1]):
        own = white[first, window, pl.ds(row, rows), :].astype(jnp.float32)
        other = white[second, window, pl.ds(row, rows), :].astype(jnp.float32)
        own_re, own_im, other_re, other_im = own[:, :bins], own[:, bins:], other[:, :bins], other[:, bins:]
        real_part = own_re * other_re + own_im * other_im
        imag_part = own_im * other_re - own_re * other_im
        real_sum = real_part if real_sum is None else real_sum + real_part
        imag_sum = imag_part if imag_sum is None else imag_sum + imag_part
    return real_sum, imag_sum


STEP = 16


def first_kernel(meta, *refs):
    pieces, (table, stack, white) = refs[:-3], refs[-3:]
    whiten(pieces, table, white)
    pairs, rows, width = stack.shape
    bins = width // 2
    for pair in range(pairs):
        first, second = meta[0, pair], meta[1, pair]

        def body(step, carry):
            row = pl.multiple_of(step * STEP, STEP)
            real_sum, imag_sum = cross(white, first, second, row, STEP)
            stack[pair, pl.ds(row, STEP), :bins] = real_sum
            stack[pair, pl.ds(row, STEP), bins:] = imag_sum
            return carry

        lax.fori_loop(0, rows // STEP, body, 0, unroll=True)


def second_kernel(rounds, meta, *refs):
    pieces = refs[: -13]
    (table, stack, counts, lag_hi, lag_lo, end_hi, end_lo, out, white, hi, lo, main, extra) = refs[-13:]
    whiten(pieces, table, white)
    pairs, rows, width = stack.shape
    bins = width // 2
    for pair in range(pairs):
        first, second = meta[0, pair], meta[1, pair]

        def body(step, carry):
            row = pl.multiple_of(step * STEP, STEP)
            real_sum, imag_sum = cross(white, first, second, row, STEP)
            real_sum = real_sum + stack[pair, pl.ds(row, STEP), :bins]
            imag_sum = imag_sum + stack[pair, pl.ds(row, STEP), bins:]
            place = pl.ds(pl.multiple_of(pair * rows + row, STEP), STEP)
            hi[place, :bins], lo[place, :bins] = split(real_sum)
            hi[place, bins:], lo[place, bins:] = split(imag_sum)
            return carry

        lax.fori_loop(0, rows // STEP, body, 0, unroll=True)
    dot = functools.partial(jnp.dot, preferred_element_type=jnp.float32)
    main[...] = dot(hi[...], lag_hi[...]) + dot(lo[...], lag_hi[...]) + dot(hi[...], lag_lo[...])
    across = functools.partial(
        lax.dot_general, dimension_numbers=(((1,), (1,)), ((), ())), preferred_element_type=jnp.float32
    )
    ends = across(end_hi[...], hi[...]) + across(end_hi[...], lo[...]) + across(end_lo[...], hi[...])
    extra[...] = counts[...]
    zones, group = out.shape[1], rows // out.shape[1]
    per_round = pairs // rounds
    for pair in range(pairs):
        step = pair // per_round
        for side in range(2):
            block = meta[2 + side, pair]
            value = main[pair * rows : (pair + 1) * rows, side * LANES : (side + 1) * LANES]
            value = value.astype(jnp.bfloat16).reshape(zones, group, LANES)
            out[block, :, step * group : (step + 1) * group, :] = value
            extra[block, step : step + 1, :rows] = ends[side : side + 1, pair * rows : (pair + 1) * rows]
    for block in range(out.shape[0]):
        tail = extra[block].astype(jnp.bfloat16)
        for zone in range(zones):
            out[block, zone, rounds * group : rounds * group + 8, :] = tail


def last_kernel(rounds, meta, parts, out):
    blocks, zones, height, _ = parts.shape
    group = out.shape[0] // blocks
    lane = lax.broadcasted_iota(jnp.int32, (group, LANES), 1)
    row = lax.broadcasted_iota(jnp.int32, (group, LANES), 0)
    chosen = lane == row + meta[4, 0]
    inverse = None
    for block in range(blocks):
        total = parts[block, 0].astype(jnp.float32)
        for zone in range(1, zones):
            total = total + parts[block, zone].astype(jnp.float32)
        tail = total[rounds * group : rounds * group + 8]
        if inverse is None:
            inverse = 1.0 / tail[rounds : 2 * rounds]
        for step in range(rounds):
            scale = inverse[step : step + 1]
            rows = slice(block * group, (block + 1) * group)
            out[rows, step, :LANES] = total[step * group : (step + 1) * group] * scale
            end = jnp.where(chosen, tail[step : step + 1] * scale, 0.0)
            out[rows, step, LANES:] = jnp.sum(end, axis=1, keepdims=True)


def by_channels(samples, valid, plan):
    chan_count, time_count = lax.axis_size("chan"), lax.axis_size("tm")
    windows, block_width, length = samples.shape
    bins = length // 2
    rounds = plan.shape[0]
    maxlag = (LAGS - 1) // 2
    zones = time_count // 2
    group = block_width // (time_count * chan_count)
    rows = zones * group
    here, now = lax.axis_index("chan"), lax.axis_index("tm")
    half = now % 2

    mask = valid.astype(jnp.float32)
    present = lax.dynamic_index_in_dim(valid, here, axis=1, keepdims=True) > 0
    grouped = samples.reshape(windows, zones, 2, chan_count, group, length)

    def piece_for(chan_step, half_step):
        place = lax.dynamic_index_in_dim(grouped, half ^ half_step, axis=2, keepdims=False)
        place = lax.dynamic_index_in_dim(place, here ^ chan_step, axis=2, keepdims=False)
        place = jnp.where(present[:, :, None, None], place, jnp.zeros((), place.dtype))
        return place.reshape(windows, rows, length)

    def partners(chan_step, half_step):
        return [
            (a * time_count + t, (a ^ chan_step) * time_count + (t ^ half_step))
            for a in range(chan_count)
            for t in range(time_count)
        ]

    received = []
    for half_step in range(2):
        for chan_step in range(chan_count):
            piece = piece_for(chan_step, half_step)
            if chan_step or half_step:
                piece = lax.ppermute(piece, ("chan", "tm"), partners(chan_step, half_step))
            received.append(piece)
    other_mask = lax.ppermute(valid, ("chan", "tm"), partners(0, 1)).astype(jnp.float32)
    masks = jnp.concatenate([mask, other_mask], axis=0)

    blocks = jnp.arange(chan_count, dtype=jnp.int32)
    leads = blocks[None, :] < plan
    order = jnp.sum(leads[:, None, :] & (blocks[None, None, :] < blocks[None, :, None]), axis=2)
    slots = jnp.arange(chan_count // 2, dtype=jnp.int32)
    chosen = (leads[:, None, :] & (order[:, None, :] == slots[None, :, None])).astype(jnp.int32)
    lead = jnp.sum(chosen * blocks[None, None, :], axis=2).reshape(-1)
    mate = jnp.sum(chosen * plan[:, None, :], axis=2).reshape(-1)
    own_rows = jnp.full_like(lead, (now // 2) * group)
    meta = jnp.stack([lead ^ here, mate ^ here, lead, mate, own_rows])
    pairs = lead.shape[0]
    same = (plan[:, :, None] == blocks[None, None, :]).astype(jnp.float32)
    partner_mask = jnp.sum(masks[:, None, None, :] * same[None], axis=3)
    counts = jnp.sum(masks[:, None, :] * partner_mask, axis=0).T
    counts = jnp.pad(counts, ((0, 0), (rounds, 8 - 2 * rounds)))
    counts = jnp.broadcast_to(counts[:, :, None], (chan_count, 8, LANES))

    table = jnp.asarray(dft_table(length, bins).astype(np.float32)).astype(jnp.bfloat16)
    shifts = np.arange(-maxlag, maxlag, dtype=np.int64)
    lags = np.concatenate([lag_table(bins, length, shifts, s) for s in (1.0, -1.0)], axis=1)
    lag_hi, lag_lo = high_low(lags)
    last = np.array([maxlag], dtype=np.int64)
    ends = np.concatenate([lag_table(bins, length, last, s) for s in (1.0, -1.0)], axis=1).T
    end_hi, end_lo = high_low(np.pad(ends, ((0, 14), (0, 0))))

    smem = pl.BlockSpec(memory_space=pltpu.SMEM)
    vmem = pl.BlockSpec(memory_space=pltpu.VMEM)
    white_shape = pltpu.VMEM((chan_count, windows, rows, length), jnp.bfloat16)
    stack = pl.pallas_call(
        first_kernel,
        out_shape=jax.ShapeDtypeStruct((pairs, rows, length), jnp.float32),
        in_specs=[smem] + [vmem] * (chan_count + 1),
        out_specs=vmem,
        scratch_shapes=[white_shape],
        name="first_half",
    )(meta, *received[:chan_count], table)
    height = rounds * group + 8
    sent = pl.pallas_call(
        functools.partial(second_kernel, rounds),
        out_shape=jax.ShapeDtypeStruct((chan_count, zones, height, LANES), jnp.bfloat16),
        in_specs=[smem] + [vmem] * (chan_count + 7),
        out_specs=vmem,
        scratch_shapes=[
            white_shape,
            pltpu.VMEM((pairs * rows, length), jnp.bfloat16),
            pltpu.VMEM((pairs * rows, length), jnp.bfloat16),
            pltpu.VMEM((pairs * rows, 2 * LANES), jnp.float32),
            pltpu.VMEM((chan_count, 8, LANES), jnp.float32),
        ],
        name="second_half",
    )(meta, *received[chan_count:], table, stack, counts, lag_hi, lag_lo, end_hi, end_lo)
    same_half = [[a * time_count + z * 2 + c for a in range(chan_count) for z in range(zones)] for c in range(2)]
    parts = lax.all_to_all(
        sent.reshape(chan_count * zones, height, LANES),
        ("chan", "tm"),
        split_axis=0,
        concat_axis=0,
        tiled=True,
        axis_index_groups=same_half,
    ).reshape(chan_count, zones, height, LANES)
    return pl.pallas_call(
        functools.partial(last_kernel, rounds),
        out_shape=jax.ShapeDtypeStruct((chan_count * group, rounds, LAGS), jnp.float32),
        in_specs=[smem, vmem],
        out_specs=vmem,
        name="finish",
    )(meta, parts)


def table_on_device(length, count):
    sample_idx = jnp.arange(length, dtype=jnp.int32)[:, None]
    bin_idx = jnp.arange(count, dtype=jnp.int32)[None, :]
    phase = (sample_idx * bin_idx % length).astype(jnp.float32) * (2.0 * math.pi / length)
    return jnp.concatenate([jnp.cos(phase), -jnp.sin(phase)], axis=1).astype(jnp.bfloat16)


def lags_on_device(first_bin, count, length, maxlag):
    bin_idx = (first_bin + jnp.arange(count, dtype=jnp.int32))[:, None]
    shifts = jnp.arange(-maxlag, maxlag + 1, dtype=jnp.int32)[None, :]
    phase = (bin_idx * shifts % length).astype(jnp.float32) * (2.0 * math.pi / length)
    return jnp.concatenate([0.25 * jnp.cos(phase), -0.25 * jnp.sin(phase)], axis=0)


def by_bins(samples, valid, plan):
    chan_count = lax.axis_size("chan")
    windows_here, block_width, length = samples.shape
    bin_count = length // 2
    share = bin_count // chan_count
    all_channels = block_width * chan_count
    rounds = plan.shape[0]
    maxlag = (LAGS - 1) // 2
    table = table_on_device(length, bin_count)
    table = (
        table.reshape(length, 2, chan_count, share)
        .transpose(0, 2, 1, 3)
        .reshape(length, 2 * bin_count)
    )
    spec = jnp.dot(samples.reshape(-1, length), table, preferred_element_type=jnp.float32)
    spec = spec.reshape(windows_here, block_width, chan_count, 2, share)
    power = spec[:, :, :, 0] * spec[:, :, :, 0] + spec[:, :, :, 1] * spec[:, :, :, 1]
    level = jnp.mean(power, axis=(2, 3), keepdims=True)
    white = spec / jnp.sqrt(power + 0.1 * level + 1e-06)[:, :, :, None, :]
    white = white.astype(jnp.bfloat16).reshape(windows_here, block_width, 2 * bin_count)
    moved = lax.all_to_all(white, "chan", split_axis=2, concat_axis=1, tiled=True)
    blocks = moved.reshape(windows_here, chan_count, block_width, 2, share)
    mask = valid.astype(jnp.float32)
    weights = jnp.stack([mask * jnp.take(mask, plan[step], axis=1) for step in range(rounds)])
    totals = lax.psum(jnp.sum(weights, axis=1), "tm")
    own = blocks.astype(jnp.float32)
    partial_list = []
    for step in range(rounds):
        other = jnp.take(blocks, plan[step], axis=1).astype(jnp.float32)
        real_part = own[:, :, :, 0] * other[:, :, :, 0] + own[:, :, :, 1] * other[:, :, :, 1]
        imag_part = own[:, :, :, 1] * other[:, :, :, 0] - own[:, :, :, 0] * other[:, :, :, 1]
        product = jnp.stack([real_part, imag_part], axis=3)
        summed = jnp.einsum("wb,wbicf->bicf", weights[step], product)
        summed = summed / totals[step][:, None, None, None]
        partial_list.append(summed.reshape(all_channels, 2 * share))
    partial_value = jnp.stack(partial_list, axis=1)
    lags = lags_on_device(lax.axis_index("chan") * share, share, length, maxlag)
    return lax.psum_scatter(
        jnp.einsum("crk,kl->crl", partial_value, lags, precision=lax.Precision.HIGHEST),
        ("chan", "tm"),
        scatter_dimension=0,
        tiled=True,
    )


def shards(samples, valid, plan):
    chan_count, time_count = lax.axis_size("chan"), lax.axis_size("tm")
    block_width = samples.shape[1]
    rows_each = block_width // (time_count * chan_count)
    whole_tiles = rows_each > 0 and rows_each % STEP == 0 and block_width == rows_each * time_count * chan_count
    powers = chan_count & (chan_count - 1) == 0 and chan_count > 1 and time_count % 2 == 0
    if whole_tiles and powers and rows_each * time_count // 2 <= LANES and 2 * plan.shape[0] <= 8:
        return by_channels(samples, valid, plan)
    return by_bins(samples, valid, plan)


def solution(mesh):
    return jax.shard_map(
        shards,
        mesh=mesh,
        in_specs=(P("tm", "chan", None), P("tm", None), P()),
        out_specs=P(("chan", "tm"), None, None),
        check_vma=False,
    )
```

```python
import functools
import math

import jax
import jax.numpy as jnp
import numpy as np
from jax import lax
from jax.experimental import pallas as pl
from jax.experimental.pallas import tpu as pltpu
from jax.sharding import PartitionSpec as P


LAGS = 129
LANES = 128


def dft_table(length, count):
    sample_idx = np.arange(length, dtype=np.int64)[:, None]
    bin_idx = np.arange(count, dtype=np.int64)[None, :]
    phase = (sample_idx * bin_idx % length).astype(np.float64) * (2.0 * math.pi / length)
    return np.concatenate([np.cos(phase), -np.sin(phase)], axis=1)


def lag_table(count, length, shifts, sign):
    bin_idx = np.arange(count, dtype=np.int64)[:, None]
    phase = (bin_idx * shifts[None, :] % length).astype(np.float64) * (2.0 * math.pi / length)
    return np.concatenate([0.25 * np.cos(phase), -0.25 * sign * np.sin(phase)], axis=0)


def high_low(table):
    high = jnp.asarray(table.astype(np.float32)).astype(jnp.bfloat16)
    low = (jnp.asarray(table.astype(np.float32)) - high.astype(jnp.float32)).astype(jnp.bfloat16)
    return high, low


def split(value):
    high = value.astype(jnp.bfloat16)
    return high, (value - high.astype(jnp.float32)).astype(jnp.bfloat16)


def whiten(pieces, keep, table, spec, white):
    windows, rows, length = pieces[0][2].shape
    bins = length // 2
    data = jnp.concatenate([piece[...].reshape(windows * rows, length) for _, _, piece in pieces], axis=0)
    spec[: data.shape[0], :] = jnp.dot(data, table[...], preferred_element_type=jnp.float32)
    for order, (half, slot, _) in enumerate(pieces):
        for window in range(windows):
            present = keep[half * windows + window, slot]
            start = (order * windows + window) * rows

            def body(step, carry):
                row = pl.multiple_of(step * STEP, STEP)
                real = spec[pl.ds(start + row, STEP), :bins]
                imag = spec[pl.ds(start + row, STEP), bins:]
                power = real * real + imag * imag
                level = jnp.mean(power, axis=1, keepdims=True)
                scale = lax.rsqrt(power + 0.1 * level + 1e-06) * present
                target = white(half, slot)
                target[window, pl.ds(row, STEP), :bins] = (real * scale).astype(jnp.bfloat16)
                target[window, pl.ds(row, STEP), bins:] = (imag * scale).astype(jnp.bfloat16)
                return carry

            lax.fori_loop(0, rows // STEP, body, 0, unroll=True)


def cross(white, first, second, row, rows):
    bins = white.shape[3] // 2
    real_sum, imag_sum = None, None
    for window in range(white.shape[1]):
        own = white[first, window, pl.ds(row, rows), :].astype(jnp.float32)
        other = white[second, window, pl.ds(row, rows), :].astype(jnp.float32)
        own_re, own_im, other_re, other_im = own[:, :bins], own[:, bins:], other[:, :bins], other[:, bins:]
        real_part = own_re * other_re + own_im * other_im
        imag_part = own_im * other_re - own_re * other_im
        real_sum = real_part if real_sum is None else real_sum + real_part
        imag_sum = imag_part if imag_sum is None else imag_sum + imag_part
    return real_sum, imag_sum


STEP = 16


def early_kernel(slots, keep, *refs):
    pieces, (table, out, spec) = refs[:-3], refs[-3:]
    place = {key: order for order, key in enumerate(slots)}
    listed = [(half, slot, piece) for (half, slot), piece in zip(slots, pieces, strict=True)]
    whiten(listed, keep, table, spec, lambda half, slot: out.at[place[half, slot]])


def gather_white(half, slots, late, early, white):
    for order, (early_half, slot) in enumerate(slots):
        if early_half == half:
            white[slot] = early[order]
    return [(half, slot, piece) for slot, piece in late]


def first_kernel(slots, late, meta, keep, *refs):
    pieces, (early, table, stack, spec, white) = refs[:-5], refs[-5:]
    listed = gather_white(0, slots, list(zip(late, pieces, strict=True)), early, white)
    whiten(listed, keep, table, spec, lambda half, slot: white.at[slot])
    pairs, rows, width = stack.shape
    bins = width // 2
    for pair in range(pairs):
        first, second = meta[0, pair], meta[1, pair]

        def body(step, carry):
            row = pl.multiple_of(step * STEP, STEP)
            real_sum, imag_sum = cross(white, first, second, row, STEP)
            stack[pair, pl.ds(row, STEP), :bins] = real_sum
            stack[pair, pl.ds(row, STEP), bins:] = imag_sum
            return carry

        lax.fori_loop(0, rows // STEP, body, 0, unroll=True)


def second_kernel(rounds, slots, late, meta, keep, *refs):
    pieces = refs[:-15]
    (early, table, stack, counts, lag_hi, lag_lo, end_hi, end_lo, out, spec, white, hi, lo, main, extra) = refs[-15:]
    listed = gather_white(1, slots, list(zip(late, pieces, strict=True)), early, white)
    whiten(listed, keep, table, spec, lambda half, slot: white.at[slot])
    pairs, rows, width = stack.shape
    bins = width // 2
    for pair in range(pairs):
        first, second = meta[0, pair], meta[1, pair]

        def body(step, carry):
            row = pl.multiple_of(step * STEP, STEP)
            real_sum, imag_sum = cross(white, first, second, row, STEP)
            real_sum = real_sum + stack[pair, pl.ds(row, STEP), :bins]
            imag_sum = imag_sum + stack[pair, pl.ds(row, STEP), bins:]
            place = pl.ds(pl.multiple_of(pair * rows + row, STEP), STEP)
            hi[place, :bins], lo[place, :bins] = split(real_sum)
            hi[place, bins:], lo[place, bins:] = split(imag_sum)
            return carry

        lax.fori_loop(0, rows // STEP, body, 0, unroll=True)
    dot = functools.partial(jnp.dot, preferred_element_type=jnp.float32)
    main[...] = dot(hi[...], lag_hi[...]) + dot(lo[...], lag_hi[...]) + dot(hi[...], lag_lo[...])
    across = functools.partial(
        lax.dot_general, dimension_numbers=(((1,), (1,)), ((), ())), preferred_element_type=jnp.float32
    )
    ends = across(end_hi[...], hi[...]) + across(end_hi[...], lo[...]) + across(end_lo[...], hi[...])
    extra[...] = counts[...]
    zones, group = out.shape[1], rows // out.shape[1]
    per_round = pairs // rounds
    for pair in range(pairs):
        step = pair // per_round
        for side in range(2):
            block = meta[2 + side, pair]
            value = main[pair * rows : (pair + 1) * rows, side * LANES : (side + 1) * LANES]
            value = value.astype(jnp.bfloat16).reshape(zones, group, LANES)
            out[block, :, step * group : (step + 1) * group, :] = value
            extra[block, step : step + 1, :rows] = ends[side : side + 1, pair * rows : (pair + 1) * rows]
    for block in range(out.shape[0]):
        tail = extra[block].astype(jnp.bfloat16)
        for zone in range(zones):
            out[block, zone, rounds * group : rounds * group + 8, :] = tail


def last_kernel(rounds, meta, parts, out):
    blocks, zones, _, _ = parts.shape
    group = out.shape[1] // blocks
    lane = lax.broadcasted_iota(jnp.int32, (group, LANES), 1)
    row = lax.broadcasted_iota(jnp.int32, (group, LANES), 0)
    chosen = lane == row + meta[4, 0]
    inverse = None
    for block in range(blocks):
        total = parts[block, 0].astype(jnp.float32)
        for zone in range(1, zones):
            total = total + parts[block, zone].astype(jnp.float32)
        tail = total[rounds * group : rounds * group + 8]
        if inverse is None:
            inverse = 1.0 / tail[rounds : 2 * rounds]
        for step in range(rounds):
            scale = inverse[step : step + 1]
            rows = slice(block * group, (block + 1) * group)
            out[step, rows, :LANES] = total[step * group : (step + 1) * group] * scale
            end = jnp.where(chosen, tail[step : step + 1] * scale, 0.0)
            out[step, rows, LANES:] = jnp.sum(end, axis=1, keepdims=True)


def by_channels(samples, valid, plan):
    chan_count, time_count = lax.axis_size("chan"), lax.axis_size("tm")
    windows, block_width, length = samples.shape
    bins = length // 2
    rounds = plan.shape[0]
    maxlag = (LAGS - 1) // 2
    zones = time_count // 2
    group = block_width // (time_count * chan_count)
    rows = zones * group
    here, now = lax.axis_index("chan"), lax.axis_index("tm")
    half = now % 2

    def piece_for(source, half_step, chan_step):
        grouped = source.reshape(windows, zones, 2, chan_count, group, length)
        place = lax.dynamic_slice(
            grouped,
            (0, 0, half ^ half_step, here ^ chan_step, 0, 0),
            (windows, zones, 1, 1, group, length),
        )
        return place.reshape(windows, rows, length)

    def partners(half_step, chan_step):
        return [
            (a * time_count + t, (a ^ chan_step) * time_count + (t ^ half_step))
            for a in range(chan_count)
            for t in range(time_count)
        ]

    def is_late(chan_step):
        return chan_step & (chan_step - 1) == 0 and chan_step > 0

    early_steps = [s for s in range(chan_count - 1, -1, -1) if not is_late(s)]
    late_steps = [s for s in range(chan_count) if is_late(s)]
    early_slots = [(h, s) for s in early_steps for h in range(2)]
    late_slots = [(h, s) for h in range(2) for s in late_steps]
    received, source, sent_pieces = {}, samples, 0
    for key in early_slots + late_slots:
        piece = piece_for(source, *key)
        if key == early_slots[0]:
            source, piece = lax.optimization_barrier((source, piece))
        if key != (0, 0):
            piece = lax.ppermute(piece, ("chan", "tm"), partners(*key))
            sent_pieces += 1
        received[key] = piece

    _, late_valid = lax.optimization_barrier((source, valid))
    other_mask = lax.ppermute(late_valid, ("chan", "tm"), partners(1, 0)).astype(jnp.float32)
    masks = jnp.concatenate([valid.astype(jnp.float32), other_mask], axis=0)

    blocks = jnp.arange(chan_count, dtype=jnp.int32)
    leads = blocks[None, :] < plan
    order = jnp.sum(leads[:, None, :] & (blocks[None, None, :] < blocks[None, :, None]), axis=2)
    slots = jnp.arange(chan_count // 2, dtype=jnp.int32)
    chosen = (leads[:, None, :] & (order[:, None, :] == slots[None, :, None])).astype(jnp.int32)
    lead = jnp.sum(chosen * blocks[None, None, :], axis=2).reshape(-1)
    mate = jnp.sum(chosen * plan[:, None, :], axis=2).reshape(-1)
    own_rows = jnp.full_like(lead, (now // 2) * group)
    meta = jnp.stack([lead ^ here, mate ^ here, lead, mate, own_rows])
    pairs = lead.shape[0]
    same = (plan[:, :, None] == blocks[None, None, :]).astype(jnp.float32)
    partner_mask = jnp.sum(masks[:, None, None, :] * same[None], axis=3)
    counts = jnp.sum(masks[:, None, :] * partner_mask, axis=0).T
    counts = jnp.pad(counts, ((0, 0), (rounds, 8 - 2 * rounds)))
    counts = jnp.broadcast_to(counts[:, :, None], (chan_count, 8, LANES))
    at_slot = (blocks[None, :] == (blocks[:, None] ^ here)).astype(jnp.float32)
    keep = jnp.sum(masks[:, None, :] * at_slot[None], axis=2)

    table = jnp.asarray(dft_table(length, bins).astype(np.float32)).astype(jnp.bfloat16)
    shifts = np.arange(-maxlag, maxlag, dtype=np.int64)
    lags = np.concatenate([lag_table(bins, length, shifts, s) for s in (1.0, -1.0)], axis=1)
    lag_hi, lag_lo = high_low(lags)
    last = np.array([maxlag], dtype=np.int64)
    ends = np.concatenate([lag_table(bins, length, last, s) for s in (1.0, -1.0)], axis=1).T
    end_hi, end_lo = high_low(np.pad(ends, ((0, 14), (0, 0))))

    smem = pl.BlockSpec(memory_space=pltpu.SMEM)
    vmem = pl.BlockSpec(memory_space=pltpu.VMEM)
    params = pltpu.CompilerParams(vmem_limit_bytes=24 * 1024 * 1024)

    def spec_scratch(pieces):
        return pltpu.VMEM((pieces * windows * rows, length), jnp.float32)

    white_scratch = pltpu.VMEM((chan_count, windows, rows, length), jnp.bfloat16)
    early = pl.pallas_call(
        functools.partial(early_kernel, early_slots),
        out_shape=jax.ShapeDtypeStruct((len(early_slots), windows, rows, length), jnp.bfloat16),
        in_specs=[smem] + [vmem] * (len(early_slots) + 1),
        out_specs=vmem,
        scratch_shapes=[spec_scratch(len(early_slots))],
        compiler_params=params,
        name="early",
    )(keep, *[received[key] for key in early_slots], table)
    stack = pl.pallas_call(
        functools.partial(first_kernel, early_slots, late_steps),
        out_shape=jax.ShapeDtypeStruct((pairs, rows, length), jnp.float32),
        in_specs=[smem] * 2 + [vmem] * (len(late_steps) + 2),
        out_specs=vmem,
        scratch_shapes=[spec_scratch(len(late_steps)), white_scratch],
        compiler_params=params,
        name="first_half",
    )(meta, keep, *[received[0, s] for s in late_steps], early, table)
    height = rounds * group + 8
    sent = pl.pallas_call(
        functools.partial(second_kernel, rounds, early_slots, late_steps),
        out_shape=jax.ShapeDtypeStruct((chan_count, zones, height, LANES), jnp.bfloat16),
        in_specs=[smem] * 2 + [vmem] * (len(late_steps) + 8),
        out_specs=vmem,
        scratch_shapes=[
            spec_scratch(len(late_steps)),
            white_scratch,
            pltpu.VMEM((pairs * rows, length), jnp.bfloat16),
            pltpu.VMEM((pairs * rows, length), jnp.bfloat16),
            pltpu.VMEM((pairs * rows, 2 * LANES), jnp.float32),
            pltpu.VMEM((chan_count, 8, LANES), jnp.float32),
        ],
        compiler_params=params,
        name="second_half",
    )(meta, keep, *[received[1, s] for s in late_steps], early, table, stack, counts, lag_hi, lag_lo, end_hi, end_lo)
    same_half = [[a * time_count + z * 2 + c for a in range(chan_count) for z in range(zones)] for c in range(2)]
    parts = lax.all_to_all(
        sent.reshape(chan_count * zones, height, LANES),
        ("chan", "tm"),
        split_axis=0,
        concat_axis=0,
        tiled=True,
        axis_index_groups=same_half,
    ).reshape(chan_count, zones, height, LANES)
    result = pl.pallas_call(
        functools.partial(last_kernel, rounds),
        out_shape=jax.ShapeDtypeStruct((rounds, chan_count * group, LAGS), jnp.float32),
        in_specs=[smem, vmem],
        out_specs=vmem,
        compiler_params=params,
        name="finish",
    )(meta, parts)
    return result.transpose(1, 0, 2)


def table_on_device(length, count):
    sample_idx = jnp.arange(length, dtype=jnp.int32)[:, None]
    bin_idx = jnp.arange(count, dtype=jnp.int32)[None, :]
    phase = (sample_idx * bin_idx % length).astype(jnp.float32) * (2.0 * math.pi / length)
    return jnp.concatenate([jnp.cos(phase), -jnp.sin(phase)], axis=1).astype(jnp.bfloat16)


def lags_on_device(first_bin, count, length, maxlag):
    bin_idx = (first_bin + jnp.arange(count, dtype=jnp.int32))[:, None]
    shifts = jnp.arange(-maxlag, maxlag + 1, dtype=jnp.int32)[None, :]
    phase = (bin_idx * shifts % length).astype(jnp.float32) * (2.0 * math.pi / length)
    return jnp.concatenate([0.25 * jnp.cos(phase), -0.25 * jnp.sin(phase)], axis=0)


def by_bins(samples, valid, plan):
    chan_count = lax.axis_size("chan")
    windows_here, block_width, length = samples.shape
    bin_count = length // 2
    share = bin_count // chan_count
    all_channels = block_width * chan_count
    rounds = plan.shape[0]
    maxlag = (LAGS - 1) // 2
    table = table_on_device(length, bin_count)
    table = (
        table.reshape(length, 2, chan_count, share)
        .transpose(0, 2, 1, 3)
        .reshape(length, 2 * bin_count)
    )
    spec = jnp.dot(samples.reshape(-1, length), table, preferred_element_type=jnp.float32)
    spec = spec.reshape(windows_here, block_width, chan_count, 2, share)
    power = spec[:, :, :, 0] * spec[:, :, :, 0] + spec[:, :, :, 1] * spec[:, :, :, 1]
    level = jnp.mean(power, axis=(2, 3), keepdims=True)
    white = spec / jnp.sqrt(power + 0.1 * level + 1e-06)[:, :, :, None, :]
    white = white.astype(jnp.bfloat16).reshape(windows_here, block_width, 2 * bin_count)
    moved = lax.all_to_all(white, "chan", split_axis=2, concat_axis=1, tiled=True)
    blocks = moved.reshape(windows_here, chan_count, block_width, 2, share)
    mask = valid.astype(jnp.float32)
    weights = jnp.stack([mask * jnp.take(mask, plan[step], axis=1) for step in range(rounds)])
    totals = lax.psum(jnp.sum(weights, axis=1), "tm")
    own = blocks.astype(jnp.float32)
    partial_list = []
    for step in range(rounds):
        other = jnp.take(blocks, plan[step], axis=1).astype(jnp.float32)
        real_part = own[:, :, :, 0] * other[:, :, :, 0] + own[:, :, :, 1] * other[:, :, :, 1]
        imag_part = own[:, :, :, 1] * other[:, :, :, 0] - own[:, :, :, 0] * other[:, :, :, 1]
        product = jnp.stack([real_part, imag_part], axis=3)
        summed = jnp.einsum("wb,wbicf->bicf", weights[step], product)
        summed = summed / totals[step][:, None, None, None]
        partial_list.append(summed.reshape(all_channels, 2 * share))
    partial_value = jnp.stack(partial_list, axis=1)
    lags = lags_on_device(lax.axis_index("chan") * share, share, length, maxlag)
    return lax.psum_scatter(
        jnp.einsum("crk,kl->crl", partial_value, lags, precision=lax.Precision.HIGHEST),
        ("chan", "tm"),
        scatter_dimension=0,
        tiled=True,
    )


def shards(samples, valid, plan):
    chan_count, time_count = lax.axis_size("chan"), lax.axis_size("tm")
    block_width = samples.shape[1]
    rows_each = block_width // (time_count * chan_count)
    whole_tiles = rows_each > 0 and rows_each % STEP == 0 and block_width == rows_each * time_count * chan_count
    powers = chan_count & (chan_count - 1) == 0 and chan_count > 1 and time_count % 2 == 0
    if whole_tiles and powers and rows_each * time_count // 2 <= LANES and 2 * plan.shape[0] <= 8:
        return by_channels(samples, valid, plan)
    return by_bins(samples, valid, plan)


def solution(mesh):
    return jax.shard_map(
        shards,
        mesh=mesh,
        in_specs=(P("tm", "chan", None), P("tm", None), P()),
        out_specs=P(("chan", "tm"), None, None),
        check_vma=False,
    )
```

```python
import functools
import math

import jax
import jax.numpy as jnp
import numpy as np
from jax import lax
from jax.experimental import pallas as pl
from jax.experimental.pallas import tpu as pltpu
from jax.sharding import PartitionSpec as P


LAGS = 129
LANES = 128
STEP = 16
PARTS = 2


def dft_table(length, count):
    sample_idx = np.arange(length, dtype=np.int64)[:, None]
    bin_idx = np.arange(count, dtype=np.int64)[None, :]
    phase = (sample_idx * bin_idx % length).astype(np.float64) * (2.0 * math.pi / length)
    return np.concatenate([np.cos(phase), -np.sin(phase)], axis=1)


def lag_table(count, length, shifts, sign):
    bin_idx = np.arange(count, dtype=np.int64)[:, None]
    phase = (bin_idx * shifts[None, :] % length).astype(np.float64) * (2.0 * math.pi / length)
    return np.concatenate([0.25 * np.cos(phase), -0.25 * sign * np.sin(phase)], axis=0)


def high_low(table):
    high = jnp.asarray(table.astype(np.float32)).astype(jnp.bfloat16)
    low = (jnp.asarray(table.astype(np.float32)) - high.astype(jnp.float32)).astype(jnp.bfloat16)
    return high, low


def split(value):
    high = value.astype(jnp.bfloat16)
    return high, (value - high.astype(jnp.float32)).astype(jnp.bfloat16)


def whiten(pieces, masks, table, spec, white):
    windows, rows, length = pieces[0][2].shape
    bins = length // 2
    data = jnp.concatenate([piece[...].reshape(windows * rows, length) for _, _, piece in pieces], axis=0)
    spec[: data.shape[0], :] = jnp.dot(data, table[...], preferred_element_type=jnp.float32)
    for order, (half, slot, _) in enumerate(pieces):
        for window in range(windows):
            present = masks[half][window, lax.axis_index("chan") ^ slot].astype(jnp.float32)
            start = (order * windows + window) * rows

            def body(step, carry):
                row = pl.multiple_of(step * STEP, STEP)
                real = spec[pl.ds(start + row, STEP), :bins]
                imag = spec[pl.ds(start + row, STEP), bins:]
                power = real * real + imag * imag
                level = jnp.mean(power, axis=1, keepdims=True)
                scale = lax.rsqrt(power + 0.1 * level + 1e-06) * present
                target = white(half, slot)
                target[window, pl.ds(row, STEP), :bins] = (real * scale).astype(jnp.bfloat16)
                target[window, pl.ds(row, STEP), bins:] = (imag * scale).astype(jnp.bfloat16)
                return carry

            lax.fori_loop(0, rows // STEP, body, 0, unroll=True)


def cross(white, first, second, row, rows):
    bins = white.shape[3] // 2
    real_sum, imag_sum = None, None
    for window in range(white.shape[1]):
        own = white[first, window, pl.ds(row, rows), :].astype(jnp.float32)
        other = white[second, window, pl.ds(row, rows), :].astype(jnp.float32)
        own_re, own_im, other_re, other_im = own[:, :bins], own[:, bins:], other[:, :bins], other[:, bins:]
        real_part = own_re * other_re + own_im * other_im
        imag_part = own_im * other_re - own_re * other_im
        real_sum = real_part if real_sum is None else real_sum + real_part
        imag_sum = imag_part if imag_sum is None else imag_sum + imag_part
    return real_sum, imag_sum


def list_pairs(plan, lead, mate):
    rounds, blocks = plan.shape
    place = 0
    for step in range(rounds):
        place = step * (blocks // 2)
        for block in range(blocks):
            partner = plan[step, block]
            lead[place] = block
            mate[place] = partner
            place = place + (partner > block).astype(jnp.int32)


def early_kernel(slots, valid, other, *refs):
    pieces, (table, out, spec) = refs[:-3], refs[-3:]
    place = {key: order for order, key in enumerate(slots)}
    listed = [(half, slot, piece) for (half, slot), piece in zip(slots, pieces, strict=True)]
    whiten(listed, (valid, other), table, spec, lambda half, slot: out.at[place[half, slot]])


def gather_white(half, slots, late, early, white):
    for order, (early_half, slot) in enumerate(slots):
        if early_half == half:
            white[slot] = early[order]
    return [(half, slot, piece) for slot, piece in late]


def first_kernel(slots, late, plan, valid, other, *refs):
    pieces, (early, table, stack, spec, white, lead, mate) = refs[:-7], refs[-7:]
    here = lax.axis_index("chan")
    list_pairs(plan, lead, mate)
    listed = gather_white(0, slots, list(zip(late, pieces, strict=True)), early, white)
    whiten(listed, (valid, other), table, spec, lambda half, slot: white.at[slot])
    pairs, rows, width = stack.shape
    bins = width // 2
    for pair in range(pairs):
        first, second = lead[pair] ^ here, mate[pair] ^ here

        def body(step, carry):
            row = pl.multiple_of(step * STEP, STEP)
            real_sum, imag_sum = cross(white, first, second, row, STEP)
            stack[pair, pl.ds(row, STEP), :bins] = real_sum
            stack[pair, pl.ds(row, STEP), bins:] = imag_sum
            return carry

        lax.fori_loop(0, rows // STEP, body, 0, unroll=True)


def second_kernel(rounds, slots, late, part, plan, valid, other, *refs):
    head, refs = refs[: len(late)], refs[len(late) :]
    done, refs = refs[:part], refs[part:]
    early, table, stack, lag_hi, lag_lo, end_hi, end_lo, out, spec, white, hi, lo, main, extra, lead, mate = refs
    here = lax.axis_index("chan")
    list_pairs(plan, lead, mate)
    rows = head[0].shape[1]
    base = part * rows
    for order, (half, slot) in enumerate(slots):
        if half == 1:
            white[slot] = early[order, :, base : base + rows, :]
    whiten([(1, slot, piece) for slot, piece in zip(late, head, strict=True)], (valid, other), table, spec, lambda half, slot: white.at[slot])
    pairs, _, width = stack.shape
    bins = width // 2
    for pair in range(pairs):
        first, second = lead[pair] ^ here, mate[pair] ^ here

        def body(step, carry):
            row = pl.multiple_of(step * STEP, STEP)
            real_sum, imag_sum = cross(white, first, second, row, STEP)
            real_sum = real_sum + stack[pair, pl.ds(base + row, STEP), :bins]
            imag_sum = imag_sum + stack[pair, pl.ds(base + row, STEP), bins:]
            place = pl.ds(pl.multiple_of(pair * rows + row, STEP), STEP)
            hi[place, :bins], lo[place, :bins] = split(real_sum)
            hi[place, bins:], lo[place, bins:] = split(imag_sum)
            return carry

        lax.fori_loop(0, rows // STEP, body, 0, unroll=True)
    dot = functools.partial(jnp.dot, preferred_element_type=jnp.float32)
    main[...] = dot(hi[...], lag_hi[...]) + dot(lo[...], lag_hi[...]) + dot(hi[...], lag_lo[...])
    across = functools.partial(
        lax.dot_general, dimension_numbers=(((1,), (1,)), ((), ())), preferred_element_type=jnp.float32
    )
    ends = across(end_hi[...], hi[...]) + across(end_hi[...], lo[...]) + across(end_lo[...], hi[...])
    extra[...] = jnp.zeros_like(extra)
    group = (out.shape[2] - 8) // rounds
    zones = rows // group
    for earlier, ref in enumerate(done):
        out[:, earlier * zones : (earlier + 1) * zones] = ref[:, earlier * zones : (earlier + 1) * zones]
    first_zone = part * zones
    per_round = pairs // rounds
    for pair in range(pairs):
        step = pair // per_round
        count = 0
        for mask in (valid, other):
            for window in range(mask.shape[0]):
                count = count + mask[window, lead[pair]] * mask[window, mate[pair]]
        count = jnp.full((1, LANES), count.astype(jnp.float32))
        for side in range(2):
            block = (lead, mate)[side][pair]
            extra[block, rounds + step : rounds + step + 1, :] = count
            value = main[pair * rows : (pair + 1) * rows, side * LANES : (side + 1) * LANES]
            value = value.astype(jnp.bfloat16).reshape(zones, group, LANES)
            out[block, first_zone : first_zone + zones, step * group : (step + 1) * group, :] = value
            extra[block, step : step + 1, :rows] = ends[side : side + 1, pair * rows : (pair + 1) * rows]
    for block in range(out.shape[0]):
        tail = extra[block].astype(jnp.bfloat16)
        for zone in range(zones):
            out[block, first_zone + zone, rounds * group : rounds * group + 8, :] = tail


def cut_kernel(keys, zone_ranges, samples, *refs):
    outs, sems = refs[: len(keys)], refs[len(keys)]
    here, half = lax.axis_index("chan"), lax.axis_index("tm") % 2
    copies = []
    for order, ((half_step, chan_step), (start, count)) in enumerate(zip(keys, zone_ranges, strict=True)):
        source = samples.at[:, start : start + count, half ^ half_step, here ^ chan_step]
        copy = pltpu.make_async_copy(source, outs[order], sems.at[order])
        copy.start()
        copies.append(copy)
    for copy in copies:
        copy.wait()


def last_kernel(rounds, per_part, parts, out):
    blocks, zones, _, _ = parts.shape
    group = out.shape[1] // blocks
    lane = lax.broadcasted_iota(jnp.int32, (group, LANES), 1)
    row = lax.broadcasted_iota(jnp.int32, (group, LANES), 0)
    chosen = lane == row + lax.axis_index("tm") // 2 % per_part * group
    inverse = None
    for block in range(blocks):
        total = parts[block, 0].astype(jnp.float32)
        for zone in range(1, zones):
            total = total + parts[block, zone].astype(jnp.float32)
        tail = total[rounds * group : rounds * group + 8]
        if inverse is None:
            inverse = 1.0 / tail[rounds : 2 * rounds]
        for step in range(rounds):
            scale = inverse[step : step + 1]
            rows = slice(block * group, (block + 1) * group)
            out[step, rows, :LANES] = total[step * group : (step + 1) * group] * scale
            end = jnp.where(chosen, tail[step : step + 1] * scale, 0.0)
            out[step, rows, LANES:] = jnp.sum(end, axis=1, keepdims=True)


def by_channels(samples, valid, plan):
    chan_count, time_count = lax.axis_size("chan"), lax.axis_size("tm")
    windows, block_width, length = samples.shape
    bins = length // 2
    rounds = plan.shape[0]
    maxlag = (LAGS - 1) // 2
    zones = time_count // 2
    group = block_width // (time_count * chan_count)
    rows = zones * group

    smem = pl.BlockSpec(memory_space=pltpu.SMEM)
    vmem = pl.BlockSpec(memory_space=pltpu.VMEM)
    params = pltpu.CompilerParams(vmem_limit_bytes=12 * 1024 * 1024)
    grouped = samples.reshape(windows, zones, 2, chan_count, group, length)

    def cut(keys, zone_ranges):
        pieces = pl.pallas_call(
            functools.partial(cut_kernel, keys, zone_ranges),
            out_shape=[
                jax.ShapeDtypeStruct((windows, count, group, length), samples.dtype) for _, count in zone_ranges
            ],
            in_specs=[pl.BlockSpec(memory_space=pltpu.HBM)],
            out_specs=[vmem] * len(keys),
            scratch_shapes=[pltpu.SemaphoreType.DMA((len(keys),))],
            compiler_params=pltpu.CompilerParams(vmem_limit_bytes=8 * 1024 * 1024),
        )(pltpu.with_memory_space_constraint(grouped, pltpu.HBM))
        return [piece.reshape(windows, count * group, length) for piece, (_, count) in zip(pieces, zone_ranges, strict=True)]

    def partners(half_step, chan_step):
        return [
            (a * time_count + t, (a ^ chan_step) * time_count + (t ^ half_step))
            for a in range(chan_count)
            for t in range(time_count)
        ]

    def is_late(chan_step):
        return chan_step & (chan_step - 1) == 0 and chan_step > 0

    early_steps = [s for s in range(chan_count - 1, -1, -1) if not is_late(s)]
    late_steps = [s for s in range(chan_count) if is_late(s)]
    early_slots = [(h, s) for s in early_steps for h in range(2)]
    late_first = [(0, s) for s in late_steps]
    late_second = [(1, s) for s in late_steps]
    per_part = zones // PARTS
    keys = early_slots + late_first + late_second * PARTS
    ranges = [(0, zones)] * (len(early_slots) + len(late_first))
    ranges += [(part * per_part, per_part) for part in range(PARTS) for _ in late_second]
    pieces = cut(keys[:1], ranges[:1])
    pieces += cut(keys[1:], ranges[1:])
    received, sent_pieces = [], 0
    for key, piece in zip(keys, pieces, strict=True):
        if key != (0, 0):
            piece = lax.ppermute(piece, ("chan", "tm"), partners(*key))
            sent_pieces += 1
        received.append(piece)
    early_pieces, received = received[: len(early_slots)], received[len(early_slots) :]
    first_pieces, second_pieces = received[: len(late_steps)], received[len(late_steps) :]

    other = lax.ppermute(valid, ("chan", "tm"), partners(1, 0))
    pairs = rounds * (chan_count // 2)
    table = jnp.asarray(dft_table(length, bins).astype(np.float32)).astype(jnp.bfloat16)
    shifts = np.arange(-maxlag, maxlag, dtype=np.int64)
    lags = np.concatenate([lag_table(bins, length, shifts, s) for s in (1.0, -1.0)], axis=1)
    lag_hi, lag_lo = high_low(lags)
    last = np.array([maxlag], dtype=np.int64)
    ends = np.concatenate([lag_table(bins, length, last, s) for s in (1.0, -1.0)], axis=1).T
    end_hi, end_lo = high_low(np.pad(ends, ((0, 14), (0, 0))))

    lists = [pltpu.SMEM((pairs + 1,), jnp.int32)] * 2

    def spec_scratch(pieces, height):
        return pltpu.VMEM((pieces * windows * height, length), jnp.float32)

    def white_scratch(height):
        return pltpu.VMEM((chan_count, windows, height, length), jnp.bfloat16)

    early = pl.pallas_call(
        functools.partial(early_kernel, early_slots),
        out_shape=jax.ShapeDtypeStruct((len(early_slots), windows, rows, length), jnp.bfloat16),
        in_specs=[smem] * 2 + [vmem] * (len(early_slots) + 1),
        out_specs=vmem,
        scratch_shapes=[spec_scratch(len(early_slots), rows)],
        compiler_params=params,
        name="early",
    )(valid, other, *early_pieces, table)
    stack = pl.pallas_call(
        functools.partial(first_kernel, early_slots, late_steps),
        out_shape=jax.ShapeDtypeStruct((pairs, rows, length), jnp.float32),
        in_specs=[smem] * 3 + [vmem] * (len(late_steps) + 2),
        out_specs=vmem,
        scratch_shapes=[spec_scratch(len(late_steps), rows), white_scratch(rows), *lists],
        compiler_params=params,
        name="first_half",
    )(plan, valid, other, *first_pieces, early, table)
    height = rounds * group + 8
    part_rows = per_part * group
    sent = []
    for part in range(PARTS):
        heads = second_pieces[part * len(late_steps) : (part + 1) * len(late_steps)]
        sent.append(
            pl.pallas_call(
                functools.partial(second_kernel, rounds, early_slots, late_steps, part),
                out_shape=jax.ShapeDtypeStruct((chan_count, zones, height, LANES), jnp.bfloat16),
                in_specs=[smem] * 3 + [vmem] * (len(late_steps) + part + 7),
                out_specs=vmem,
                scratch_shapes=[
                    spec_scratch(len(late_steps), part_rows),
                    white_scratch(part_rows),
                    pltpu.VMEM((pairs * part_rows, length), jnp.bfloat16),
                    pltpu.VMEM((pairs * part_rows, length), jnp.bfloat16),
                    pltpu.VMEM((pairs * part_rows, 2 * LANES), jnp.float32),
                    pltpu.VMEM((chan_count, 8, LANES), jnp.float32),
                    *lists,
                ],
                compiler_params=params,
            )(plan, valid, other, *heads, *sent, early, table, stack, lag_hi, lag_lo, end_hi, end_lo)
        )
    sent = sent[-1]
    same_half = [[a * time_count + z * 2 + c for a in range(chan_count) for z in range(zones)] for c in range(2)]
    parts = lax.all_to_all(
        sent.reshape(chan_count * zones, height, LANES),
        ("chan", "tm"),
        split_axis=0,
        concat_axis=0,
        tiled=True,
        axis_index_groups=same_half,
    ).reshape(chan_count, zones, height, LANES)
    result = pl.pallas_call(
        functools.partial(last_kernel, rounds, per_part),
        out_shape=jax.ShapeDtypeStruct((rounds, chan_count * group, LAGS), jnp.float32),
        in_specs=[vmem],
        out_specs=vmem,
        compiler_params=params,
        name="finish",
    )(parts)
    return result.transpose(1, 0, 2)


def table_on_device(length, count):
    sample_idx = jnp.arange(length, dtype=jnp.int32)[:, None]
    bin_idx = jnp.arange(count, dtype=jnp.int32)[None, :]
    phase = (sample_idx * bin_idx % length).astype(jnp.float32) * (2.0 * math.pi / length)
    return jnp.concatenate([jnp.cos(phase), -jnp.sin(phase)], axis=1).astype(jnp.bfloat16)


def lags_on_device(first_bin, count, length, maxlag):
    bin_idx = (first_bin + jnp.arange(count, dtype=jnp.int32))[:, None]
    shifts = jnp.arange(-maxlag, maxlag + 1, dtype=jnp.int32)[None, :]
    phase = (bin_idx * shifts % length).astype(jnp.float32) * (2.0 * math.pi / length)
    return jnp.concatenate([0.25 * jnp.cos(phase), -0.25 * jnp.sin(phase)], axis=0)


def by_bins(samples, valid, plan):
    chan_count = lax.axis_size("chan")
    windows_here, block_width, length = samples.shape
    bin_count = length // 2
    share = bin_count // chan_count
    all_channels = block_width * chan_count
    rounds = plan.shape[0]
    maxlag = (LAGS - 1) // 2
    table = table_on_device(length, bin_count)
    table = (
        table.reshape(length, 2, chan_count, share)
        .transpose(0, 2, 1, 3)
        .reshape(length, 2 * bin_count)
    )
    spec = jnp.dot(samples.reshape(-1, length), table, preferred_element_type=jnp.float32)
    spec = spec.reshape(windows_here, block_width, chan_count, 2, share)
    power = spec[:, :, :, 0] * spec[:, :, :, 0] + spec[:, :, :, 1] * spec[:, :, :, 1]
    level = jnp.mean(power, axis=(2, 3), keepdims=True)
    white = spec / jnp.sqrt(power + 0.1 * level + 1e-06)[:, :, :, None, :]
    white = white.astype(jnp.bfloat16).reshape(windows_here, block_width, 2 * bin_count)
    moved = lax.all_to_all(white, "chan", split_axis=2, concat_axis=1, tiled=True)
    blocks = moved.reshape(windows_here, chan_count, block_width, 2, share)
    mask = valid.astype(jnp.float32)
    weights = jnp.stack([mask * jnp.take(mask, plan[step], axis=1) for step in range(rounds)])
    totals = lax.psum(jnp.sum(weights, axis=1), "tm")
    own = blocks.astype(jnp.float32)
    partial_list = []
    for step in range(rounds):
        other = jnp.take(blocks, plan[step], axis=1).astype(jnp.float32)
        real_part = own[:, :, :, 0] * other[:, :, :, 0] + own[:, :, :, 1] * other[:, :, :, 1]
        imag_part = own[:, :, :, 1] * other[:, :, :, 0] - own[:, :, :, 0] * other[:, :, :, 1]
        product = jnp.stack([real_part, imag_part], axis=3)
        summed = jnp.einsum("wb,wbicf->bicf", weights[step], product)
        summed = summed / totals[step][:, None, None, None]
        partial_list.append(summed.reshape(all_channels, 2 * share))
    partial_value = jnp.stack(partial_list, axis=1)
    lags = lags_on_device(lax.axis_index("chan") * share, share, length, maxlag)
    return lax.psum_scatter(
        jnp.einsum("crk,kl->crl", partial_value, lags, precision=lax.Precision.HIGHEST),
        ("chan", "tm"),
        scatter_dimension=0,
        tiled=True,
    )


def shards(samples, valid, plan):
    chan_count, time_count = lax.axis_size("chan"), lax.axis_size("tm")
    block_width = samples.shape[1]
    rows_each = block_width // (time_count * chan_count)
    whole_tiles = rows_each > 0 and rows_each % STEP == 0 and block_width == rows_each * time_count * chan_count
    whole_tiles = whole_tiles and time_count % (2 * PARTS) == 0
    powers = chan_count & (chan_count - 1) == 0 and chan_count > 1 and time_count % 2 == 0
    if whole_tiles and powers and rows_each * time_count // 2 <= LANES and 2 * plan.shape[0] <= 8:
        return by_channels(samples, valid, plan)
    return by_bins(samples, valid, plan)


def solution(mesh):
    return jax.shard_map(
        shards,
        mesh=mesh,
        in_specs=(P("tm", "chan", None), P("tm", None), P()),
        out_specs=P(("chan", "tm"), None, None),
        check_vma=False,
    )
```

```python
import functools
import math

import jax
import jax.numpy as jnp
import numpy as np
from jax import lax
from jax.experimental import pallas as pl
from jax.experimental.pallas import tpu as pltpu
from jax.sharding import PartitionSpec as P


LAGS = 129
LANES = 128
STEP = 16
PARTS = 2


def dft_table(length, count):
    sample_idx = np.arange(length, dtype=np.int64)[:, None]
    bin_idx = np.arange(count, dtype=np.int64)[None, :]
    phase = (sample_idx * bin_idx % length).astype(np.float64) * (2.0 * math.pi / length)
    return np.concatenate([np.cos(phase), -np.sin(phase)], axis=1)


def lag_table(count, length, shifts, sign):
    bin_idx = np.arange(count, dtype=np.int64)[:, None]
    phase = (bin_idx * shifts[None, :] % length).astype(np.float64) * (2.0 * math.pi / length)
    return np.concatenate([0.25 * np.cos(phase), -0.25 * sign * np.sin(phase)], axis=0)


def high_low(table):
    high = jnp.asarray(table.astype(np.float32)).astype(jnp.bfloat16)
    low = (jnp.asarray(table.astype(np.float32)) - high.astype(jnp.float32)).astype(jnp.bfloat16)
    return high, low


def split(value):
    high = value.astype(jnp.bfloat16)
    return high, (value - high.astype(jnp.float32)).astype(jnp.bfloat16)


def whiten(pieces, table, spec):
    length = pieces[0][0].shape[2]
    bins = length // 2
    data = jnp.concatenate([piece[...].reshape(-1, length) for piece, _, _ in pieces], axis=0)
    spec[: data.shape[0], :] = jnp.dot(data, table[...], preferred_element_type=jnp.float32)
    start = 0
    for piece, target, present in pieces:
        windows, rows, _ = piece.shape
        for window in range(windows):
            keep = present(window).astype(jnp.float32)
            for row in range(0, rows, STEP):
                real = spec[start + row : start + row + STEP, :bins]
                imag = spec[start + row : start + row + STEP, bins:]
                power = real * real + imag * imag
                level = jnp.mean(power, axis=1, keepdims=True)
                scale = lax.rsqrt(power + 0.1 * level + 1e-06) * keep
                target[window, row : row + STEP, :bins] = (real * scale).astype(jnp.bfloat16)
                target[window, row : row + STEP, bins:] = (imag * scale).astype(jnp.bfloat16)
            start += rows


def sent_kernel(count, valid, *refs):
    pieces, table, outs, spec = refs[:count], refs[count], refs[count + 1 : -1], refs[-1]
    here = lax.axis_index("chan")
    whiten([(piece, out, lambda window: valid[window, here]) for piece, out in zip(pieces, outs, strict=True)], table, spec)


def early_kernel(slots, valid, other, *refs):
    pieces, (table, out, spec) = refs[:-3], refs[-3:]
    here = lax.axis_index("chan")
    listed = []
    for order, ((half, slot), piece) in enumerate(zip(slots, pieces, strict=True)):
        mask = (valid, other)[half]
        listed.append((piece, out.at[order], lambda window, mask=mask, slot=slot: mask[window, here ^ slot]))
    whiten(listed, table, spec)


def slot_pairs(slots):
    return [(first, second) for first in range(slots) for second in range(first + 1, slots)]


def load_slots(sources, row, lane, bins):
    values = {}
    for slot, (ref, base) in sources.items():
        for window in range(ref.shape[0]):
            rows = slice(base + row, base + row + STEP)
            real = ref[window, rows, lane : lane + LANES].astype(jnp.float32)
            imag = ref[window, rows, bins + lane : bins + lane + LANES].astype(jnp.float32)
            values[slot, window] = (real, imag)
    return values


def cross(values, windows, first, second, real_sum=None, imag_sum=None):
    for window in range(windows):
        (own_re, own_im), (other_re, other_im) = values[first, window], values[second, window]
        real_part = own_re * other_re + own_im * other_im
        imag_part = own_im * other_re - own_re * other_im
        real_sum = real_part if real_sum is None else real_sum + real_part
        imag_sum = imag_part if imag_sum is None else imag_sum + imag_part
    return real_sum, imag_sum


def first_kernel(early_slots, late, *refs):
    pieces, early, stack = refs[: len(late)], refs[len(late)], refs[len(late) + 1]
    sources = {slot: (piece, 0) for slot, piece in zip(late, pieces, strict=True)}
    sources.update({slot: (early.at[order], 0) for order, (half, slot) in enumerate(early_slots) if half == 0})
    ready = {slot: (early.at[order], 0) for order, (half, slot) in enumerate(early_slots) if half == 1}
    windows = early.shape[1]
    _, rows, width = stack.shape
    bins = width // 2
    for row in range(0, rows, STEP):
        for lane in range(0, bins, LANES):
            values = load_slots(sources, row, lane, bins)
            more = load_slots(ready, row, lane, bins)
            for pair, (first, second) in enumerate(slot_pairs(len(sources))):
                sums = cross(values, windows, first, second)
                if first in ready and second in ready:
                    sums = cross(more, windows, first, second, *sums)
                stack[pair, row : row + STEP, lane : lane + LANES] = sums[0]
                stack[pair, row : row + STEP, bins + lane : bins + lane + LANES] = sums[1]


def second_kernel(rounds, early_slots, late, part, plan, valid, other, *refs):
    head, refs = refs[: len(late)], refs[len(late) :]
    done, refs = refs[:part], refs[part:]
    early, stack, lag_hi, lag_lo, out, both, main, extra = refs
    here = lax.axis_index("chan")
    windows, rows, width = head[0].shape
    base = part * rows
    bins = width // 2
    ready = {slot: (early.at[order], base) for order, (half, slot) in enumerate(early_slots) if half == 1}
    sources = {slot: (piece, 0) for slot, piece in zip(late, head, strict=True)}
    sources.update(ready)
    pairs = slot_pairs(len(sources))
    height = len(pairs) * rows
    for row in range(0, rows, STEP):
        for lane in range(0, bins, LANES):
            values = load_slots(sources, row, lane, bins)
            for pair, (first, second) in enumerate(pairs):
                lanes = (slice(lane, lane + LANES), slice(bins + lane, bins + lane + LANES))
                sums = [stack[pair, base + row : base + row + STEP, where] for where in lanes]
                if not (first in ready and second in ready):
                    sums = cross(values, windows, first, second, *sums)
                start = pair * rows + row
                for where, value in zip(lanes, sums, strict=True):
                    high, low = split(value)
                    both[start : start + STEP, where] = high
                    both[height + start : height + start + STEP, where] = low
    dot = functools.partial(jnp.dot, preferred_element_type=jnp.float32)
    double = dot(both[...], lag_hi[...])
    main[...] = double[:height] + double[height:] + dot(both[:height, :], lag_lo[...])
    extra[...] = jnp.zeros_like(extra)
    group = (out.shape[2] - 8) // rounds
    zones = rows // group
    for earlier, ref in enumerate(done):
        out[:, earlier * zones : (earlier + 1) * zones] = ref[:, earlier * zones : (earlier + 1) * zones]
    first_zone = part * zones
    diagonal = lax.broadcasted_iota(jnp.int32, (rows, LANES), 0) == lax.broadcasted_iota(jnp.int32, (rows, LANES), 1)
    for pair, slots in enumerate(pairs):
        blocks = [slot ^ here for slot in slots]
        step = 0
        for turn in range(1, rounds):
            step = step + turn * (plan[turn, blocks[0]] == blocks[1]).astype(jnp.int32)
        count = 0
        for mask in (valid, other):
            for window in range(mask.shape[0]):
                count = count + mask[window, blocks[0]] * mask[window, blocks[1]]
        count = jnp.full((1, LANES), count.astype(jnp.float32))
        place = pl.ds(pl.multiple_of(step * group, group), group)
        for side in range(2):
            value = main[pair * rows : (pair + 1) * rows, side * LANES : (side + 1) * LANES]
            value = value.astype(jnp.bfloat16).reshape(zones, group, LANES)
            out[blocks[side], first_zone : first_zone + zones, place, :] = value
            mirror = main[pair * rows : (pair + 1) * rows, (1 - side) * LANES : (1 - side) * LANES + 1]
            end = jnp.sum(jnp.where(diagonal, mirror, 0.0), axis=0, keepdims=True)
            extra[blocks[side], pl.ds(step, 1), :] = end
            extra[blocks[side], pl.ds(rounds + step, 1), :] = count
    for block in range(out.shape[0]):
        tail = extra[block].astype(jnp.bfloat16)
        for zone in range(zones):
            out[block, first_zone + zone, rounds * group : rounds * group + 8, :] = tail


def cut_kernel(keys, zone_ranges, samples, *refs):
    outs, sems = refs[: len(keys)], refs[len(keys)]
    here, half = lax.axis_index("chan"), lax.axis_index("tm") % 2
    copies = []
    for order, ((half_step, chan_step), (start, count)) in enumerate(zip(keys, zone_ranges, strict=True)):
        source = samples.at[:, start : start + count, half ^ half_step, here ^ chan_step]
        copy = pltpu.make_async_copy(source, outs[order], sems.at[order])
        copy.start()
        copies.append(copy)
    for copy in copies:
        copy.wait()


def last_kernel(rounds, per_part, parts, out):
    blocks, zones, _, _ = parts.shape
    group = out.shape[1] // blocks
    lane = lax.broadcasted_iota(jnp.int32, (group, LANES), 1)
    row = lax.broadcasted_iota(jnp.int32, (group, LANES), 0)
    chosen = lane == row + lax.axis_index("tm") // 2 % per_part * group
    inverse = None
    for block in range(blocks):
        total = parts[block, 0].astype(jnp.float32)
        for zone in range(1, zones):
            total = total + parts[block, zone].astype(jnp.float32)
        tail = total[rounds * group : rounds * group + 8]
        if inverse is None:
            inverse = 1.0 / tail[rounds : 2 * rounds]
        for step in range(rounds):
            scale = inverse[step : step + 1]
            rows = slice(block * group, (block + 1) * group)
            out[step, rows, :LANES] = total[step * group : (step + 1) * group] * scale
            end = jnp.where(chosen, tail[step : step + 1] * scale, 0.0)
            out[step, rows, LANES:] = jnp.sum(end, axis=1, keepdims=True)


def by_channels(samples, valid, plan):
    chan_count, time_count = lax.axis_size("chan"), lax.axis_size("tm")
    windows, block_width, length = samples.shape
    bins = length // 2
    rounds = plan.shape[0]
    maxlag = (LAGS - 1) // 2
    zones = time_count // 2
    group = block_width // (time_count * chan_count)
    rows = zones * group

    smem = pl.BlockSpec(memory_space=pltpu.SMEM)
    vmem = pl.BlockSpec(memory_space=pltpu.VMEM)
    params = pltpu.CompilerParams(vmem_limit_bytes=12 * 1024 * 1024)
    grouped = samples.reshape(windows, zones, 2, chan_count, group, length)

    def cut(keys, zone_ranges):
        pieces = pl.pallas_call(
            functools.partial(cut_kernel, keys, zone_ranges),
            out_shape=[
                jax.ShapeDtypeStruct((windows, count, group, length), samples.dtype) for _, count in zone_ranges
            ],
            in_specs=[pl.BlockSpec(memory_space=pltpu.HBM)],
            out_specs=[vmem] * len(keys),
            scratch_shapes=[pltpu.SemaphoreType.DMA((len(keys),))],
            compiler_params=pltpu.CompilerParams(vmem_limit_bytes=8 * 1024 * 1024),
        )(pltpu.with_memory_space_constraint(grouped, pltpu.HBM))
        return [piece.reshape(windows, count * group, length) for piece, (_, count) in zip(pieces, zone_ranges, strict=True)]

    def partners(half_step, chan_step):
        return [
            (a * time_count + t, (a ^ chan_step) * time_count + (t ^ half_step))
            for a in range(chan_count)
            for t in range(time_count)
        ]

    def is_late(chan_step):
        return chan_step & (chan_step - 1) == 0 and chan_step > 0

    early_steps = [s for s in range(chan_count - 1, -1, -1) if not is_late(s)]
    late_steps = [s for s in range(chan_count) if is_late(s)]
    early_slots = [(h, s) for s in early_steps for h in range(2)]
    late_first = [(0, s) for s in late_steps]
    late_second = [(1, s) for s in late_steps]
    per_part = zones // PARTS
    keys = early_slots + late_first + late_second * PARTS
    ranges = [(0, zones)] * (len(early_slots) + len(late_first))
    ranges += [(part * per_part, per_part) for part in range(PARTS) for _ in late_second]
    pieces = cut(keys[:1], ranges[:1])
    pieces += cut(keys[1:], ranges[1:])
    table = jnp.asarray(dft_table(length, bins).astype(np.float32)).astype(jnp.bfloat16)
    raw, late_raw = pieces[: len(early_slots)], pieces[len(early_slots) :]
    late_white = pl.pallas_call(
        functools.partial(sent_kernel, len(late_raw)),
        out_shape=[jax.ShapeDtypeStruct(piece.shape, jnp.bfloat16) for piece in late_raw],
        in_specs=[smem] + [vmem] * (len(late_raw) + 1),
        out_specs=[vmem] * len(late_raw),
        scratch_shapes=[pltpu.VMEM((2 * len(late_steps) * windows * rows, length), jnp.float32)],
        compiler_params=params,
        name="whiten_sent",
    )(valid, *late_raw, table)
    received, sent_pieces = [], 0
    for key, piece in zip(keys, [*raw, *late_white], strict=True):
        if key != (0, 0):
            piece = lax.ppermute(piece, ("chan", "tm"), partners(*key))
            sent_pieces += 1
        received.append(piece)
    early_pieces, received = received[: len(early_slots)], received[len(early_slots) :]
    first_pieces, second_pieces = received[: len(late_steps)], received[len(late_steps) :]

    other = lax.ppermute(valid, ("chan", "tm"), partners(1, 0))
    pairs = len(slot_pairs(chan_count))
    shifts = np.arange(-maxlag, maxlag, dtype=np.int64)
    lags = np.concatenate([lag_table(bins, length, shifts, s) for s in (1.0, -1.0)], axis=1)
    lag_hi, lag_lo = high_low(lags)

    early = pl.pallas_call(
        functools.partial(early_kernel, early_slots),
        out_shape=jax.ShapeDtypeStruct((len(early_slots), windows, rows, length), jnp.bfloat16),
        in_specs=[smem] * 2 + [vmem] * (len(early_slots) + 1),
        out_specs=vmem,
        scratch_shapes=[pltpu.VMEM((len(early_slots) * windows * rows, length), jnp.float32)],
        compiler_params=params,
        name="early",
    )(valid, other, *early_pieces, table)
    stack = pl.pallas_call(
        functools.partial(first_kernel, early_slots, late_steps),
        out_shape=jax.ShapeDtypeStruct((pairs, rows, length), jnp.float32),
        in_specs=[vmem] * (len(late_steps) + 1),
        out_specs=vmem,
        compiler_params=params,
        name="first_half",
    )(*first_pieces, early)
    height = rounds * group + 8
    part_rows = per_part * group
    sent = []
    for part in range(PARTS):
        heads = second_pieces[part * len(late_steps) : (part + 1) * len(late_steps)]
        sent.append(
            pl.pallas_call(
                functools.partial(second_kernel, rounds, early_slots, late_steps, part),
                out_shape=jax.ShapeDtypeStruct((chan_count, zones, height, LANES), jnp.bfloat16),
                in_specs=[smem] * 3 + [vmem] * (len(late_steps) + part + 4),
                out_specs=vmem,
                scratch_shapes=[
                    pltpu.VMEM((2 * pairs * part_rows, length), jnp.bfloat16),
                    pltpu.VMEM((pairs * part_rows, 2 * LANES), jnp.float32),
                    pltpu.VMEM((chan_count, 8, LANES), jnp.float32),
                ],
                compiler_params=params,
            )(plan, valid, other, *heads, *sent, early, stack, lag_hi, lag_lo)
        )
    sent = sent[-1]
    same_half = [[a * time_count + z * 2 + c for a in range(chan_count) for z in range(zones)] for c in range(2)]
    parts = lax.all_to_all(
        sent.reshape(chan_count * zones, height, LANES),
        ("chan", "tm"),
        split_axis=0,
        concat_axis=0,
        tiled=True,
        axis_index_groups=same_half,
    ).reshape(chan_count, zones, height, LANES)
    result = pl.pallas_call(
        functools.partial(last_kernel, rounds, per_part),
        out_shape=jax.ShapeDtypeStruct((rounds, chan_count * group, LAGS), jnp.float32),
        in_specs=[vmem],
        out_specs=vmem,
        compiler_params=params,
        name="finish",
    )(parts)
    return result.transpose(1, 0, 2)


def table_on_device(length, count):
    sample_idx = jnp.arange(length, dtype=jnp.int32)[:, None]
    bin_idx = jnp.arange(count, dtype=jnp.int32)[None, :]
    phase = (sample_idx * bin_idx % length).astype(jnp.float32) * (2.0 * math.pi / length)
    return jnp.concatenate([jnp.cos(phase), -jnp.sin(phase)], axis=1).astype(jnp.bfloat16)


def lags_on_device(first_bin, count, length, maxlag):
    bin_idx = (first_bin + jnp.arange(count, dtype=jnp.int32))[:, None]
    shifts = jnp.arange(-maxlag, maxlag + 1, dtype=jnp.int32)[None, :]
    phase = (bin_idx * shifts % length).astype(jnp.float32) * (2.0 * math.pi / length)
    return jnp.concatenate([0.25 * jnp.cos(phase), -0.25 * jnp.sin(phase)], axis=0)


def by_bins(samples, valid, plan):
    chan_count = lax.axis_size("chan")
    windows_here, block_width, length = samples.shape
    bin_count = length // 2
    share = bin_count // chan_count
    all_channels = block_width * chan_count
    rounds = plan.shape[0]
    maxlag = (LAGS - 1) // 2
    table = table_on_device(length, bin_count)
    table = (
        table.reshape(length, 2, chan_count, share)
        .transpose(0, 2, 1, 3)
        .reshape(length, 2 * bin_count)
    )
    spec = jnp.dot(samples.reshape(-1, length), table, preferred_element_type=jnp.float32)
    spec = spec.reshape(windows_here, block_width, chan_count, 2, share)
    power = spec[:, :, :, 0] * spec[:, :, :, 0] + spec[:, :, :, 1] * spec[:, :, :, 1]
    level = jnp.mean(power, axis=(2, 3), keepdims=True)
    white = spec / jnp.sqrt(power + 0.1 * level + 1e-06)[:, :, :, None, :]
    white = white.astype(jnp.bfloat16).reshape(windows_here, block_width, 2 * bin_count)
    moved = lax.all_to_all(white, "chan", split_axis=2, concat_axis=1, tiled=True)
    blocks = moved.reshape(windows_here, chan_count, block_width, 2, share)
    mask = valid.astype(jnp.float32)
    weights = jnp.stack([mask * jnp.take(mask, plan[step], axis=1) for step in range(rounds)])
    totals = lax.psum(jnp.sum(weights, axis=1), "tm")
    own = blocks.astype(jnp.float32)
    partial_list = []
    for step in range(rounds):
        other = jnp.take(blocks, plan[step], axis=1).astype(jnp.float32)
        real_part = own[:, :, :, 0] * other[:, :, :, 0] + own[:, :, :, 1] * other[:, :, :, 1]
        imag_part = own[:, :, :, 1] * other[:, :, :, 0] - own[:, :, :, 0] * other[:, :, :, 1]
        product = jnp.stack([real_part, imag_part], axis=3)
        summed = jnp.einsum("wb,wbicf->bicf", weights[step], product)
        summed = summed / totals[step][:, None, None, None]
        partial_list.append(summed.reshape(all_channels, 2 * share))
    partial_value = jnp.stack(partial_list, axis=1)
    lags = lags_on_device(lax.axis_index("chan") * share, share, length, maxlag)
    return lax.psum_scatter(
        jnp.einsum("crk,kl->crl", partial_value, lags, precision=lax.Precision.HIGHEST),
        ("chan", "tm"),
        scatter_dimension=0,
        tiled=True,
    )


def shards(samples, valid, plan):
    chan_count, time_count = lax.axis_size("chan"), lax.axis_size("tm")
    block_width = samples.shape[1]
    rows_each = block_width // (time_count * chan_count)
    whole_tiles = rows_each > 0 and rows_each % STEP == 0 and block_width == rows_each * time_count * chan_count
    whole_tiles = whole_tiles and time_count % (2 * PARTS) == 0 and plan.shape[0] == chan_count - 1
    powers = chan_count & (chan_count - 1) == 0 and chan_count > 1 and time_count % 2 == 0
    if whole_tiles and powers and rows_each * time_count // 2 <= LANES and 2 * plan.shape[0] <= 8:
        return by_channels(samples, valid, plan)
    return by_bins(samples, valid, plan)


def solution(mesh):
    return jax.shard_map(
        shards,
        mesh=mesh,
        in_specs=(P("tm", "chan", None), P("tm", None), P()),
        out_specs=P(("chan", "tm"), None, None),
        check_vma=False,
    )
```

```python
import functools
import math

import jax
import jax.numpy as jnp
import numpy as np
from jax import lax
from jax.experimental import pallas as pl
from jax.experimental.pallas import tpu as pltpu
from jax.sharding import PartitionSpec as P


LAGS = 129
LANES = 128
STEP = 16
PARTS = 4


def dft_table(length, count):
    sample_idx = np.arange(length, dtype=np.int64)[:, None]
    bin_idx = np.arange(count, dtype=np.int64)[None, :]
    phase = (sample_idx * bin_idx % length).astype(np.float64) * (2.0 * math.pi / length)
    return np.concatenate([np.cos(phase), -np.sin(phase)], axis=1)


def lag_table(count, length, shifts, sign):
    bin_idx = np.arange(count, dtype=np.int64)[:, None]
    phase = (bin_idx * shifts[None, :] % length).astype(np.float64) * (2.0 * math.pi / length)
    return np.concatenate([0.25 * np.cos(phase), -0.25 * sign * np.sin(phase)], axis=0)


def high_low(table):
    high = jnp.asarray(table.astype(np.float32)).astype(jnp.bfloat16)
    low = (jnp.asarray(table.astype(np.float32)) - high.astype(jnp.float32)).astype(jnp.bfloat16)
    return high, low


def split(value):
    high = value.astype(jnp.bfloat16)
    return high, (value - high.astype(jnp.float32)).astype(jnp.bfloat16)


def whiten(pieces, table, spec):
    length = pieces[0][0].shape[2]
    bins = length // 2
    data = jnp.concatenate([piece[...].reshape(-1, length) for piece, _, _ in pieces], axis=0)
    spec[: data.shape[0], :] = jnp.dot(data, table[...], preferred_element_type=jnp.float32)
    start = 0
    for piece, target, present in pieces:
        windows, rows, _ = piece.shape
        for window in range(windows):
            keep = present(window).astype(jnp.float32)
            for row in range(0, rows, STEP):
                real = spec[start + row : start + row + STEP, :bins]
                imag = spec[start + row : start + row + STEP, bins:]
                power = real * real + imag * imag
                level = jnp.mean(power, axis=1, keepdims=True)
                scale = lax.rsqrt(power + 0.1 * level + 1e-06) * keep
                target[window, row : row + STEP, :bins] = (real * scale).astype(jnp.bfloat16)
                target[window, row : row + STEP, bins:] = (imag * scale).astype(jnp.bfloat16)
            start += rows


def sent_kernel(count, valid, *refs):
    pieces, table, outs, spec = refs[:count], refs[count], refs[count + 1 : -1], refs[-1]
    here = lax.axis_index("chan")
    whiten([(piece, out, lambda window: valid[window, here]) for piece, out in zip(pieces, outs, strict=True)], table, spec)


def early_kernel(slots, plan, valid, other, *refs):
    pieces, (table, out, tails, order, spec) = refs[:-5], refs[-5:]
    here = lax.axis_index("chan")
    rounds, blocks = plan.shape
    tails[...] = jnp.zeros_like(tails)
    for block in range(blocks):
        for step in range(1, blocks):
            count = 0
            for mask in (valid, other):
                for window in range(mask.shape[0]):
                    count = count + mask[window, block] * mask[window, block ^ step]
            tails[block, rounds + step - 1 : rounds + step, :] = jnp.full((1, LANES), count.astype(jnp.float32))
    for turn in range(rounds):
        for step in range(1, blocks):
            met = (plan[turn, here] == here ^ step).astype(jnp.float32)
            order[turn, step - 1 : step, :] = jnp.full((1, LANES), met)
    listed = []
    for number, ((half, slot), piece) in enumerate(zip(slots, pieces, strict=True)):
        mask = (valid, other)[half]
        listed.append((piece, out.at[number], lambda window, mask=mask, slot=slot: mask[window, here ^ slot]))
    whiten(listed, table, spec)


def slot_pairs(slots):
    return [(first, second) for first in range(slots) for second in range(first + 1, slots)]


def load_slots(sources, row, lane, bins):
    values = {}
    for slot, (ref, base) in sources.items():
        for window in range(ref.shape[0]):
            rows = slice(base + row, base + row + STEP)
            real = ref[window, rows, lane : lane + LANES].astype(jnp.float32)
            imag = ref[window, rows, bins + lane : bins + lane + LANES].astype(jnp.float32)
            values[slot, window] = (real, imag)
    return values


def cross(values, windows, first, second, real_sum=None, imag_sum=None):
    for window in range(windows):
        (own_re, own_im), (other_re, other_im) = values[first, window], values[second, window]
        real_part = own_re * other_re + own_im * other_im
        imag_part = own_im * other_re - own_re * other_im
        real_sum = real_part if real_sum is None else real_sum + real_part
        imag_sum = imag_part if imag_sum is None else imag_sum + imag_part
    return real_sum, imag_sum


def first_kernel(early_slots, late, *refs):
    pieces, early, stack = refs[: len(late)], refs[len(late)], refs[len(late) + 1]
    sources = {slot: (piece, 0) for slot, piece in zip(late, pieces, strict=True)}
    sources.update({slot: (early.at[order], 0) for order, (half, slot) in enumerate(early_slots) if half == 0})
    ready = {slot: (early.at[order], 0) for order, (half, slot) in enumerate(early_slots) if half == 1}
    windows = early.shape[1]
    _, rows, width = stack.shape
    bins = width // 2
    for row in range(0, rows, STEP):
        for lane in range(0, bins, LANES):
            values = load_slots(sources, row, lane, bins)
            more = load_slots(ready, row, lane, bins)
            for pair, (first, second) in enumerate(slot_pairs(len(sources))):
                sums = cross(values, windows, first, second)
                if first in ready and second in ready:
                    sums = cross(more, windows, first, second, *sums)
                stack[pair, row : row + STEP, lane : lane + LANES] = sums[0]
                stack[pair, row : row + STEP, bins + lane : bins + lane + LANES] = sums[1]


def second_kernel(rounds, early_slots, late, part, *refs):
    head, refs = refs[: len(late)], refs[len(late) :]
    done, refs = refs[:part], refs[part:]
    early, stack, tails, lag_hi, lag_lo, out, both, main, extra = refs
    here = lax.axis_index("chan")
    windows, rows, width = head[0].shape
    base = part * rows
    bins = width // 2
    ready = {slot: (early.at[order], base) for order, (half, slot) in enumerate(early_slots) if half == 1}
    sources = {slot: (piece, 0) for slot, piece in zip(late, head, strict=True)}
    sources.update(ready)
    pairs = slot_pairs(len(sources))
    height = len(pairs) * rows
    for row in range(0, rows, STEP):
        for lane in range(0, bins, LANES):
            values = load_slots(sources, row, lane, bins)
            for pair, (first, second) in enumerate(pairs):
                lanes = (slice(lane, lane + LANES), slice(bins + lane, bins + lane + LANES))
                sums = [stack[pair, base + row : base + row + STEP, where] for where in lanes]
                if not (first in ready and second in ready):
                    sums = cross(values, windows, first, second, *sums)
                start = pair * rows + row
                for where, value in zip(lanes, sums, strict=True):
                    high, low = split(value)
                    both[start : start + STEP, where] = high
                    both[height + start : height + start + STEP, where] = low
    dot = functools.partial(jnp.dot, preferred_element_type=jnp.float32)
    double = dot(both[...], lag_hi[...])
    main[...] = double[:height] + double[height:] + dot(both[:height, :], lag_lo[...])
    extra[...] = tails[...]
    group = (out.shape[2] - 8) // rounds
    zones = rows // group
    for earlier, ref in enumerate(done):
        out[:, earlier * zones : (earlier + 1) * zones] = ref[:, earlier * zones : (earlier + 1) * zones]
    first_zone = part * zones
    diagonal = lax.broadcasted_iota(jnp.int32, (rows, LANES), 0) == lax.broadcasted_iota(jnp.int32, (rows, LANES), 1)
    for pair, slots in enumerate(pairs):
        blocks = [slot ^ here for slot in slots]
        step = (slots[0] ^ slots[1]) - 1
        for side in range(2):
            value = main[pair * rows : (pair + 1) * rows, side * LANES : (side + 1) * LANES]
            value = value.astype(jnp.bfloat16).reshape(zones, group, LANES)
            out[blocks[side], first_zone : first_zone + zones, step * group : (step + 1) * group, :] = value
            mirror = main[pair * rows : (pair + 1) * rows, (1 - side) * LANES : (1 - side) * LANES + 1]
            end = jnp.sum(jnp.where(diagonal, mirror, 0.0), axis=0, keepdims=True)
            extra[blocks[side], step : step + 1, :] = end
    for block in range(out.shape[0]):
        tail = extra[block].astype(jnp.bfloat16)
        for zone in range(zones):
            out[block, first_zone + zone, rounds * group : rounds * group + 8, :] = tail


def cut_kernel(keys, zone_ranges, samples, *refs):
    outs, sems = refs[: len(keys)], refs[len(keys)]
    here, half = lax.axis_index("chan"), lax.axis_index("tm") % 2
    copies = []
    for order, ((half_step, chan_step), (start, count)) in enumerate(zip(keys, zone_ranges, strict=True)):
        source = samples.at[:, start : start + count, half ^ half_step, here ^ chan_step]
        copy = pltpu.make_async_copy(source, outs[order], sems.at[order])
        copy.start()
        copies.append(copy)
    for copy in copies:
        copy.wait()


def last_kernel(rounds, per_part, parts, order, out):
    blocks, zones, _, _ = parts.shape
    group = out.shape[1] // blocks
    lane = lax.broadcasted_iota(jnp.int32, (group, LANES), 1)
    row = lax.broadcasted_iota(jnp.int32, (group, LANES), 0)
    chosen = lane == row + lax.axis_index("tm") // 2 % per_part * group
    inverse = None
    for block in range(blocks):
        total = parts[block, 0].astype(jnp.float32)
        for zone in range(1, zones):
            total = total + parts[block, zone].astype(jnp.float32)
        tail = total[rounds * group : rounds * group + 8]
        if inverse is None:
            inverse = 1.0 / tail[rounds : 2 * rounds]
        values, ends = [], []
        for step in range(rounds):
            scale = inverse[step : step + 1]
            values.append(total[step * group : (step + 1) * group] * scale)
            end = jnp.where(chosen, tail[step : step + 1] * scale, 0.0)
            ends.append(jnp.sum(end, axis=1, keepdims=True))
        rows = slice(block * group, (block + 1) * group)
        for turn in range(rounds):
            value, end = values[0], ends[0]
            for step in range(1, rounds):
                met = order[turn, step : step + 1, :] > 0.5
                value = jnp.where(met, values[step], value)
                end = jnp.where(met[:, :1], ends[step], end)
            out[turn, rows, :LANES] = value
            out[turn, rows, LANES:] = end


def by_channels(samples, valid, plan):
    chan_count, time_count = lax.axis_size("chan"), lax.axis_size("tm")
    windows, block_width, length = samples.shape
    bins = length // 2
    rounds = plan.shape[0]
    maxlag = (LAGS - 1) // 2
    zones = time_count // 2
    group = block_width // (time_count * chan_count)
    rows = zones * group

    smem = pl.BlockSpec(memory_space=pltpu.SMEM)
    vmem = pl.BlockSpec(memory_space=pltpu.VMEM)
    params = pltpu.CompilerParams(vmem_limit_bytes=12 * 1024 * 1024)
    grouped = samples.reshape(windows, zones, 2, chan_count, group, length)

    def cut(keys, zone_ranges):
        pieces = pl.pallas_call(
            functools.partial(cut_kernel, keys, zone_ranges),
            out_shape=[
                jax.ShapeDtypeStruct((windows, count, group, length), samples.dtype) for _, count in zone_ranges
            ],
            in_specs=[pl.BlockSpec(memory_space=pltpu.HBM)],
            out_specs=[vmem] * len(keys),
            scratch_shapes=[pltpu.SemaphoreType.DMA((len(keys),))],
            compiler_params=pltpu.CompilerParams(vmem_limit_bytes=8 * 1024 * 1024),
        )(pltpu.with_memory_space_constraint(grouped, pltpu.HBM))
        return [piece.reshape(windows, count * group, length) for piece, (_, count) in zip(pieces, zone_ranges, strict=True)]

    def partners(half_step, chan_step):
        return [
            (a * time_count + t, (a ^ chan_step) * time_count + (t ^ half_step))
            for a in range(chan_count)
            for t in range(time_count)
        ]

    def is_late(chan_step):
        return chan_step & (chan_step - 1) == 0 and chan_step > 0

    early_steps = [s for s in range(chan_count - 1, -1, -1) if not is_late(s)]
    late_steps = [s for s in range(chan_count) if is_late(s)]
    early_slots = [(h, s) for s in early_steps for h in range(2)]
    late_first = [(0, s) for s in late_steps]
    late_second = [(1, s) for s in late_steps]
    per_part = zones // PARTS
    keys = early_slots + late_first + late_second * PARTS
    ranges = [(0, zones)] * (len(early_slots) + len(late_first))
    ranges += [(part * per_part, per_part) for part in range(PARTS) for _ in late_second]
    pieces = cut(keys[:1], ranges[:1])
    pieces += cut(keys[1:], ranges[1:])
    table = jnp.asarray(dft_table(length, bins).astype(np.float32)).astype(jnp.bfloat16)
    raw, late_raw = pieces[: len(early_slots)], pieces[len(early_slots) :]
    late_white = pl.pallas_call(
        functools.partial(sent_kernel, len(late_raw)),
        out_shape=[jax.ShapeDtypeStruct(piece.shape, jnp.bfloat16) for piece in late_raw],
        in_specs=[smem] + [vmem] * (len(late_raw) + 1),
        out_specs=[vmem] * len(late_raw),
        scratch_shapes=[pltpu.VMEM((2 * len(late_steps) * windows * rows, length), jnp.float32)],
        compiler_params=params,
        name="whiten_sent",
    )(valid, *late_raw, table)
    received, sent_pieces = [], 0
    for key, piece in zip(keys, [*raw, *late_white], strict=True):
        if key != (0, 0):
            piece = lax.ppermute(piece, ("chan", "tm"), partners(*key))
            sent_pieces += 1
        received.append(piece)
    early_pieces, received = received[: len(early_slots)], received[len(early_slots) :]
    first_pieces, second_pieces = received[: len(late_steps)], received[len(late_steps) :]

    other = lax.ppermute(valid, ("chan", "tm"), partners(1, 0))
    pairs = len(slot_pairs(chan_count))
    shifts = np.arange(-maxlag, maxlag, dtype=np.int64)
    lags = np.concatenate([lag_table(bins, length, shifts, s) for s in (1.0, -1.0)], axis=1)
    lag_hi, lag_lo = high_low(lags)

    early, tails, order = pl.pallas_call(
        functools.partial(early_kernel, early_slots),
        out_shape=[
            jax.ShapeDtypeStruct((len(early_slots), windows, rows, length), jnp.bfloat16),
            jax.ShapeDtypeStruct((chan_count, 8, LANES), jnp.float32),
            jax.ShapeDtypeStruct((rounds, 8, LANES), jnp.float32),
        ],
        in_specs=[smem] * 3 + [vmem] * (len(early_slots) + 1),
        out_specs=[vmem] * 3,
        scratch_shapes=[pltpu.VMEM((len(early_slots) * windows * rows, length), jnp.float32)],
        compiler_params=params,
        name="early",
    )(plan, valid, other, *early_pieces, table)
    stack = pl.pallas_call(
        functools.partial(first_kernel, early_slots, late_steps),
        out_shape=jax.ShapeDtypeStruct((pairs, rows, length), jnp.float32),
        in_specs=[vmem] * (len(late_steps) + 1),
        out_specs=vmem,
        compiler_params=params,
        name="first_half",
    )(*first_pieces, early)
    height = rounds * group + 8
    part_rows = per_part * group
    sent = []
    for part in range(PARTS):
        heads = second_pieces[part * len(late_steps) : (part + 1) * len(late_steps)]
        sent.append(
            pl.pallas_call(
                functools.partial(second_kernel, rounds, early_slots, late_steps, part),
                out_shape=jax.ShapeDtypeStruct((chan_count, zones, height, LANES), jnp.bfloat16),
                in_specs=[vmem] * (len(late_steps) + part + 5),
                out_specs=vmem,
                scratch_shapes=[
                    pltpu.VMEM((2 * pairs * part_rows, length), jnp.bfloat16),
                    pltpu.VMEM((pairs * part_rows, 2 * LANES), jnp.float32),
                    pltpu.VMEM((chan_count, 8, LANES), jnp.float32),
                ],
                compiler_params=params,
            )(*heads, *sent, early, stack, tails, lag_hi, lag_lo)
        )
    sent = sent[-1]
    same_half = [[a * time_count + z * 2 + c for a in range(chan_count) for z in range(zones)] for c in range(2)]
    parts = lax.all_to_all(
        sent.reshape(chan_count * zones, height, LANES),
        ("chan", "tm"),
        split_axis=0,
        concat_axis=0,
        tiled=True,
        axis_index_groups=same_half,
    ).reshape(chan_count, zones, height, LANES)
    result = pl.pallas_call(
        functools.partial(last_kernel, rounds, per_part),
        out_shape=jax.ShapeDtypeStruct((rounds, chan_count * group, LAGS), jnp.float32),
        in_specs=[vmem] * 2,
        out_specs=vmem,
        compiler_params=params,
        name="finish",
    )(parts, order)
    return result.transpose(1, 0, 2)


def table_on_device(length, count):
    sample_idx = jnp.arange(length, dtype=jnp.int32)[:, None]
    bin_idx = jnp.arange(count, dtype=jnp.int32)[None, :]
    phase = (sample_idx * bin_idx % length).astype(jnp.float32) * (2.0 * math.pi / length)
    return jnp.concatenate([jnp.cos(phase), -jnp.sin(phase)], axis=1).astype(jnp.bfloat16)


def lags_on_device(first_bin, count, length, maxlag):
    bin_idx = (first_bin + jnp.arange(count, dtype=jnp.int32))[:, None]
    shifts = jnp.arange(-maxlag, maxlag + 1, dtype=jnp.int32)[None, :]
    phase = (bin_idx * shifts % length).astype(jnp.float32) * (2.0 * math.pi / length)
    return jnp.concatenate([0.25 * jnp.cos(phase), -0.25 * jnp.sin(phase)], axis=0)


def by_bins(samples, valid, plan):
    chan_count = lax.axis_size("chan")
    windows_here, block_width, length = samples.shape
    bin_count = length // 2
    share = bin_count // chan_count
    all_channels = block_width * chan_count
    rounds = plan.shape[0]
    maxlag = (LAGS - 1) // 2
    table = table_on_device(length, bin_count)
    table = (
        table.reshape(length, 2, chan_count, share)
        .transpose(0, 2, 1, 3)
        .reshape(length, 2 * bin_count)
    )
    spec = jnp.dot(samples.reshape(-1, length), table, preferred_element_type=jnp.float32)
    spec = spec.reshape(windows_here, block_width, chan_count, 2, share)
    power = spec[:, :, :, 0] * spec[:, :, :, 0] + spec[:, :, :, 1] * spec[:, :, :, 1]
    level = jnp.mean(power, axis=(2, 3), keepdims=True)
    white = spec / jnp.sqrt(power + 0.1 * level + 1e-06)[:, :, :, None, :]
    white = white.astype(jnp.bfloat16).reshape(windows_here, block_width, 2 * bin_count)
    moved = lax.all_to_all(white, "chan", split_axis=2, concat_axis=1, tiled=True)
    blocks = moved.reshape(windows_here, chan_count, block_width, 2, share)
    mask = valid.astype(jnp.float32)
    weights = jnp.stack([mask * jnp.take(mask, plan[step], axis=1) for step in range(rounds)])
    totals = lax.psum(jnp.sum(weights, axis=1), "tm")
    own = blocks.astype(jnp.float32)
    partial_list = []
    for step in range(rounds):
        other = jnp.take(blocks, plan[step], axis=1).astype(jnp.float32)
        real_part = own[:, :, :, 0] * other[:, :, :, 0] + own[:, :, :, 1] * other[:, :, :, 1]
        imag_part = own[:, :, :, 1] * other[:, :, :, 0] - own[:, :, :, 0] * other[:, :, :, 1]
        product = jnp.stack([real_part, imag_part], axis=3)
        summed = jnp.einsum("wb,wbicf->bicf", weights[step], product)
        summed = summed / totals[step][:, None, None, None]
        partial_list.append(summed.reshape(all_channels, 2 * share))
    partial_value = jnp.stack(partial_list, axis=1)
    lags = lags_on_device(lax.axis_index("chan") * share, share, length, maxlag)
    return lax.psum_scatter(
        jnp.einsum("crk,kl->crl", partial_value, lags, precision=lax.Precision.HIGHEST),
        ("chan", "tm"),
        scatter_dimension=0,
        tiled=True,
    )


def shards(samples, valid, plan):
    chan_count, time_count = lax.axis_size("chan"), lax.axis_size("tm")
    block_width = samples.shape[1]
    rows_each = block_width // (time_count * chan_count)
    whole_tiles = rows_each > 0 and rows_each % STEP == 0 and block_width == rows_each * time_count * chan_count
    whole_tiles = whole_tiles and time_count % (2 * PARTS) == 0 and plan.shape[0] == chan_count - 1
    powers = chan_count & (chan_count - 1) == 0 and chan_count > 1 and time_count % 2 == 0
    if whole_tiles and powers and rows_each * time_count // 2 <= LANES and 2 * plan.shape[0] <= 8:
        return by_channels(samples, valid, plan)
    return by_bins(samples, valid, plan)


def solution(mesh):
    return jax.shard_map(
        shards,
        mesh=mesh,
        in_specs=(P("tm", "chan", None), P("tm", None), P()),
        out_specs=P(("chan", "tm"), None, None),
        check_vma=False,
    )
```

```python
import functools
import math

import jax
import jax.numpy as jnp
import numpy as np
from jax import lax
from jax.experimental import pallas as pl
from jax.experimental.pallas import tpu as pltpu
from jax.sharding import PartitionSpec as P


LAGS = 129
LANES = 128
STEP = 16
PARTS = 4


def dft_table(length, count):
    sample_idx = np.arange(length, dtype=np.int64)[:, None]
    bin_idx = np.arange(count, dtype=np.int64)[None, :]
    phase = (sample_idx * bin_idx % length).astype(np.float64) * (2.0 * math.pi / length)
    return np.concatenate([np.cos(phase), -np.sin(phase)], axis=1)


def lag_table(count, length, shifts, sign):
    bin_idx = np.arange(count, dtype=np.int64)[:, None]
    phase = (bin_idx * shifts[None, :] % length).astype(np.float64) * (2.0 * math.pi / length)
    return np.concatenate([0.25 * np.cos(phase), -0.25 * sign * np.sin(phase)], axis=0)


def high_low(table):
    high = jnp.asarray(table.astype(np.float32)).astype(jnp.bfloat16)
    low = (jnp.asarray(table.astype(np.float32)) - high.astype(jnp.float32)).astype(jnp.bfloat16)
    return high, low


def split(value):
    high = value.astype(jnp.bfloat16)
    return high, (value - high.astype(jnp.float32)).astype(jnp.bfloat16)


def whiten(pieces, table, spec):
    length = pieces[0][0].shape[2]
    bins = length // 2
    data = jnp.concatenate([piece[...].reshape(-1, length) for piece, _, _ in pieces], axis=0)
    spec[: data.shape[0], :] = jnp.dot(data, table[...], preferred_element_type=jnp.float32)
    start = 0
    for piece, target, present in pieces:
        windows, rows, _ = piece.shape
        for window in range(windows):
            keep = present(window).astype(jnp.float32)
            for row in range(0, rows, STEP):
                real = spec[start + row : start + row + STEP, :bins]
                imag = spec[start + row : start + row + STEP, bins:]
                power = real * real + imag * imag
                level = jnp.mean(power, axis=1, keepdims=True)
                scale = lax.rsqrt(power + 0.1 * level + 1e-06) * keep
                target[window, row : row + STEP, :bins] = (real * scale).astype(jnp.bfloat16)
                target[window, row : row + STEP, bins:] = (imag * scale).astype(jnp.bfloat16)
            start += rows


def sent_kernel(count, valid, *refs):
    pieces, table, outs, spec = refs[:count], refs[count], refs[count + 1 : -1], refs[-1]
    here = lax.axis_index("chan")
    whiten([(piece, out, lambda window: valid[window, here]) for piece, out in zip(pieces, outs, strict=True)], table, spec)


def early_kernel(slots, plan, valid, other, *refs):
    pieces, (table, out, tails, order, spec) = refs[:-5], refs[-5:]
    here = lax.axis_index("chan")
    rounds, blocks = plan.shape
    tails[...] = jnp.zeros_like(tails)
    for block in range(blocks):
        for step in range(1, blocks):
            count = 0
            for mask in (valid, other):
                for window in range(mask.shape[0]):
                    count = count + mask[window, block] * mask[window, block ^ step]
            tails[block, rounds + step - 1 : rounds + step, :] = jnp.full((1, LANES), count.astype(jnp.float32))
    for turn in range(rounds):
        for step in range(1, blocks):
            met = (plan[turn, here] == here ^ step).astype(jnp.float32)
            order[turn, step - 1 : step, :] = jnp.full((1, LANES), met)
    listed = []
    for number, ((half, slot), piece) in enumerate(zip(slots, pieces, strict=True)):
        mask = (valid, other)[half]
        listed.append((piece, out.at[number], lambda window, mask=mask, slot=slot: mask[window, here ^ slot]))
    whiten(listed, table, spec)


def slot_pairs(slots):
    return [(first, second) for first in range(slots) for second in range(first + 1, slots)]


def load_slots(sources, row, lane, bins):
    values = {}
    for slot, (ref, base) in sources.items():
        for window in range(ref.shape[0]):
            rows = slice(base + row, base + row + STEP)
            real = ref[window, rows, lane : lane + LANES].astype(jnp.float32)
            imag = ref[window, rows, bins + lane : bins + lane + LANES].astype(jnp.float32)
            values[slot, window] = (real, imag)
    return values


def cross(values, windows, first, second, real_sum=None, imag_sum=None):
    for window in range(windows):
        (own_re, own_im), (other_re, other_im) = values[first, window], values[second, window]
        real_part = own_re * other_re + own_im * other_im
        imag_part = own_im * other_re - own_re * other_im
        real_sum = real_part if real_sum is None else real_sum + real_part
        imag_sum = imag_part if imag_sum is None else imag_sum + imag_part
    return real_sum, imag_sum


def first_kernel(early_slots, late, *refs):
    pieces, early, stack = refs[: len(late)], refs[len(late)], refs[len(late) + 1]
    sources = {slot: (piece, 0) for slot, piece in zip(late, pieces, strict=True)}
    sources.update({slot: (early.at[order], 0) for order, (half, slot) in enumerate(early_slots) if half == 0})
    ready = {slot: (early.at[order], 0) for order, (half, slot) in enumerate(early_slots) if half == 1}
    windows = early.shape[1]
    _, rows, width = stack.shape
    bins = width // 2
    for row in range(0, rows, STEP):
        for lane in range(0, bins, LANES):
            values = load_slots(sources, row, lane, bins)
            more = load_slots(ready, row, lane, bins)
            for pair, (first, second) in enumerate(slot_pairs(len(sources))):
                sums = cross(values, windows, first, second)
                if first in ready and second in ready:
                    sums = cross(more, windows, first, second, *sums)
                stack[pair, row : row + STEP, lane : lane + LANES] = sums[0]
                stack[pair, row : row + STEP, bins + lane : bins + lane + LANES] = sums[1]


def second_kernel(rounds, early_slots, late, part, *refs):
    head, refs = refs[: len(late)], refs[len(late) :]
    done, refs = refs[:part], refs[part:]
    early, stack, tails, lag_hi, lag_lo, out, both, main, extra = refs
    here = lax.axis_index("chan")
    windows, rows, width = head[0].shape
    base = part * rows
    bins = width // 2
    ready = {slot: (early.at[order], base) for order, (half, slot) in enumerate(early_slots) if half == 1}
    sources = {slot: (piece, 0) for slot, piece in zip(late, head, strict=True)}
    sources.update(ready)
    pairs = slot_pairs(len(sources))
    height = len(pairs) * rows
    for row in range(0, rows, STEP):
        for lane in range(0, bins, LANES):
            values = load_slots(sources, row, lane, bins)
            for pair, (first, second) in enumerate(pairs):
                lanes = (slice(lane, lane + LANES), slice(bins + lane, bins + lane + LANES))
                sums = [stack[pair, base + row : base + row + STEP, where] for where in lanes]
                if not (first in ready and second in ready):
                    sums = cross(values, windows, first, second, *sums)
                start = pair * rows + row
                for where, value in zip(lanes, sums, strict=True):
                    high, low = split(value)
                    both[start : start + STEP, where] = high
                    both[height + start : height + start + STEP, where] = low
    dot = functools.partial(jnp.dot, preferred_element_type=jnp.float32)
    double = dot(both[...], lag_hi[...])
    main[...] = double[:height] + double[height:] + dot(both[:height, :], lag_lo[...])
    extra[...] = tails[...]
    group = (out.shape[2] - 8) // rounds
    zones = rows // group
    first_zone = out.shape[1] - (part + 1) * zones
    for earlier, ref in enumerate(done):
        start = out.shape[1] - (earlier + 1) * zones
        out[:, start : start + zones] = ref[:, start : start + zones]
    diagonal = lax.broadcasted_iota(jnp.int32, (rows, LANES), 0) == lax.broadcasted_iota(jnp.int32, (rows, LANES), 1)
    for pair, slots in enumerate(pairs):
        blocks = [slot ^ here for slot in slots]
        step = (slots[0] ^ slots[1]) - 1
        for side in range(2):
            value = main[pair * rows : (pair + 1) * rows, side * LANES : (side + 1) * LANES]
            value = value.astype(jnp.bfloat16).reshape(zones, group, LANES)
            for zone in range(zones):
                place = first_zone + zones - 1 - zone
                out[blocks[side], place, step * group : (step + 1) * group, :] = value[zone]
            mirror = main[pair * rows : (pair + 1) * rows, (1 - side) * LANES : (1 - side) * LANES + 1]
            end = jnp.sum(jnp.where(diagonal, mirror, 0.0), axis=0, keepdims=True)
            extra[blocks[side], step : step + 1, :] = end
    for block in range(out.shape[0]):
        tail = extra[block].astype(jnp.bfloat16)
        for zone in range(zones):
            out[block, first_zone + zone, rounds * group : rounds * group + 8, :] = tail


def cut_kernel(keys, zone_ranges, samples, *refs):
    outs, sems = refs[: len(keys)], refs[len(keys)]
    here, half = lax.axis_index("chan"), lax.axis_index("tm") % 2
    copies = []
    for order, ((half_step, chan_step), (start, count)) in enumerate(zip(keys, zone_ranges, strict=True)):
        source = samples.at[:, start : start + count, half ^ half_step, here ^ chan_step]
        copy = pltpu.make_async_copy(source, outs[order], sems.at[order])
        copy.start()
        copies.append(copy)
    for copy in copies:
        copy.wait()


def last_kernel(rounds, per_part, parts, order, out):
    blocks, zones, _, _ = parts.shape
    group = out.shape[1] // blocks
    lane = lax.broadcasted_iota(jnp.int32, (group, LANES), 1)
    row = lax.broadcasted_iota(jnp.int32, (group, LANES), 0)
    chosen = lane == row + lax.axis_index("tm") // 2 % per_part * group
    inverse = None
    for block in range(blocks):
        total = parts[block, 0].astype(jnp.float32)
        for zone in range(1, zones):
            total = total + parts[block, zone].astype(jnp.float32)
        tail = total[rounds * group : rounds * group + 8]
        if inverse is None:
            inverse = 1.0 / tail[rounds : 2 * rounds]
        values, ends = [], []
        for step in range(rounds):
            scale = inverse[step : step + 1]
            values.append(total[step * group : (step + 1) * group] * scale)
            end = jnp.where(chosen, tail[step : step + 1] * scale, 0.0)
            ends.append(jnp.sum(end, axis=1, keepdims=True))
        rows = slice(block * group, (block + 1) * group)
        for turn in range(rounds):
            value, end = values[0], ends[0]
            for step in range(1, rounds):
                met = order[turn, step : step + 1, :] > 0.5
                value = jnp.where(met, values[step], value)
                end = jnp.where(met[:, :1], ends[step], end)
            out[turn, rows, :LANES] = value
            out[turn, rows, LANES:] = end


def by_channels(samples, valid, plan):
    chan_count, time_count = lax.axis_size("chan"), lax.axis_size("tm")
    windows, block_width, length = samples.shape
    bins = length // 2
    rounds = plan.shape[0]
    maxlag = (LAGS - 1) // 2
    zones = time_count // 2
    group = block_width // (time_count * chan_count)
    rows = zones * group

    smem = pl.BlockSpec(memory_space=pltpu.SMEM)
    vmem = pl.BlockSpec(memory_space=pltpu.VMEM)
    params = pltpu.CompilerParams(vmem_limit_bytes=12 * 1024 * 1024)
    grouped = samples.reshape(windows, zones, 2, chan_count, group, length)

    def cut(keys, zone_ranges):
        pieces = pl.pallas_call(
            functools.partial(cut_kernel, keys, zone_ranges),
            out_shape=[
                jax.ShapeDtypeStruct((windows, count, group, length), samples.dtype) for _, count in zone_ranges
            ],
            in_specs=[pl.BlockSpec(memory_space=pltpu.HBM)],
            out_specs=[vmem] * len(keys),
            scratch_shapes=[pltpu.SemaphoreType.DMA((len(keys),))],
            compiler_params=pltpu.CompilerParams(vmem_limit_bytes=8 * 1024 * 1024),
        )(pltpu.with_memory_space_constraint(grouped, pltpu.HBM))
        return [piece.reshape(windows, count * group, length) for piece, (_, count) in zip(pieces, zone_ranges, strict=True)]

    def partners(half_step, chan_step):
        return [
            (a * time_count + t, (a ^ chan_step) * time_count + (t ^ half_step))
            for a in range(chan_count)
            for t in range(time_count)
        ]

    def is_late(chan_step):
        return chan_step & (chan_step - 1) == 0 and chan_step > 0

    early_steps = [s for s in range(chan_count - 1, -1, -1) if not is_late(s)]
    late_steps = [s for s in range(chan_count) if is_late(s)]
    early_slots = [(h, s) for s in early_steps for h in range(2)]
    late_first = [(0, s) for s in late_steps]
    late_second = [(1, s) for s in late_steps]
    per_part = zones // PARTS
    keys = early_slots + late_first + late_second * PARTS
    ranges = [(0, zones)] * (len(early_slots) + len(late_first))
    ranges += [(part * per_part, per_part) for part in range(PARTS) for _ in late_second]
    pieces = cut(keys[:1], ranges[:1])
    pieces += cut(keys[1:], ranges[1:])
    table = jnp.asarray(dft_table(length, bins).astype(np.float32)).astype(jnp.bfloat16)
    raw, late_raw = pieces[: len(early_slots)], pieces[len(early_slots) :]
    late_white = pl.pallas_call(
        functools.partial(sent_kernel, len(late_raw)),
        out_shape=[jax.ShapeDtypeStruct(piece.shape, jnp.bfloat16) for piece in late_raw],
        in_specs=[smem] + [vmem] * (len(late_raw) + 1),
        out_specs=[vmem] * len(late_raw),
        scratch_shapes=[pltpu.VMEM((2 * len(late_steps) * windows * rows, length), jnp.float32)],
        compiler_params=params,
        name="whiten_sent",
    )(valid, *late_raw, table)
    received, sent_pieces = [], 0
    for key, piece in zip(keys, [*raw, *late_white], strict=True):
        if key != (0, 0):
            piece = lax.ppermute(piece, ("chan", "tm"), partners(*key))
            sent_pieces += 1
        received.append(piece)
    early_pieces, received = received[: len(early_slots)], received[len(early_slots) :]
    first_pieces, second_pieces = received[: len(late_steps)], received[len(late_steps) :]

    other = lax.ppermute(valid, ("chan", "tm"), partners(1, 0))
    pairs = len(slot_pairs(chan_count))
    shifts = np.arange(-maxlag, maxlag, dtype=np.int64)
    lags = np.concatenate([lag_table(bins, length, shifts, s) for s in (1.0, -1.0)], axis=1)
    lag_hi, lag_lo = high_low(lags)

    early, tails, order = pl.pallas_call(
        functools.partial(early_kernel, early_slots),
        out_shape=[
            jax.ShapeDtypeStruct((len(early_slots), windows, rows, length), jnp.bfloat16),
            jax.ShapeDtypeStruct((chan_count, 8, LANES), jnp.float32),
            jax.ShapeDtypeStruct((rounds, 8, LANES), jnp.float32),
        ],
        in_specs=[smem] * 3 + [vmem] * (len(early_slots) + 1),
        out_specs=[vmem] * 3,
        scratch_shapes=[pltpu.VMEM((len(early_slots) * windows * rows, length), jnp.float32)],
        compiler_params=params,
        name="early",
    )(plan, valid, other, *early_pieces, table)
    stack = pl.pallas_call(
        functools.partial(first_kernel, early_slots, late_steps),
        out_shape=jax.ShapeDtypeStruct((pairs, rows, length), jnp.float32),
        in_specs=[vmem] * (len(late_steps) + 1),
        out_specs=vmem,
        compiler_params=params,
        name="first_half",
    )(*first_pieces, early)
    height = rounds * group + 8
    part_rows = per_part * group
    sent = []
    for part in range(PARTS):
        heads = second_pieces[part * len(late_steps) : (part + 1) * len(late_steps)]
        sent.append(
            pl.pallas_call(
                functools.partial(second_kernel, rounds, early_slots, late_steps, part),
                out_shape=jax.ShapeDtypeStruct((chan_count, zones, height, LANES), jnp.bfloat16),
                in_specs=[vmem] * (len(late_steps) + part + 5),
                out_specs=vmem,
                scratch_shapes=[
                    pltpu.VMEM((2 * pairs * part_rows, length), jnp.bfloat16),
                    pltpu.VMEM((pairs * part_rows, 2 * LANES), jnp.float32),
                    pltpu.VMEM((chan_count, 8, LANES), jnp.float32),
                ],
                compiler_params=params,
            )(*heads, *sent, early, stack, tails, lag_hi, lag_lo)
        )
    sent = sent[-1]
    same_half = [[a * time_count + z * 2 + c for a in range(chan_count) for z in reversed(range(zones))] for c in range(2)]
    parts = lax.all_to_all(
        sent.reshape(chan_count * zones, height, LANES),
        ("chan", "tm"),
        split_axis=0,
        concat_axis=0,
        tiled=True,
        axis_index_groups=same_half,
    ).reshape(chan_count, zones, height, LANES)
    result = pl.pallas_call(
        functools.partial(last_kernel, rounds, per_part),
        out_shape=jax.ShapeDtypeStruct((rounds, chan_count * group, LAGS), jnp.float32),
        in_specs=[vmem] * 2,
        out_specs=vmem,
        compiler_params=params,
        name="finish",
    )(parts, order)
    return result.transpose(1, 0, 2)


def table_on_device(length, count):
    sample_idx = jnp.arange(length, dtype=jnp.int32)[:, None]
    bin_idx = jnp.arange(count, dtype=jnp.int32)[None, :]
    phase = (sample_idx * bin_idx % length).astype(jnp.float32) * (2.0 * math.pi / length)
    return jnp.concatenate([jnp.cos(phase), -jnp.sin(phase)], axis=1).astype(jnp.bfloat16)


def lags_on_device(first_bin, count, length, maxlag):
    bin_idx = (first_bin + jnp.arange(count, dtype=jnp.int32))[:, None]
    shifts = jnp.arange(-maxlag, maxlag + 1, dtype=jnp.int32)[None, :]
    phase = (bin_idx * shifts % length).astype(jnp.float32) * (2.0 * math.pi / length)
    return jnp.concatenate([0.25 * jnp.cos(phase), -0.25 * jnp.sin(phase)], axis=0)


def by_bins(samples, valid, plan):
    chan_count = lax.axis_size("chan")
    windows_here, block_width, length = samples.shape
    bin_count = length // 2
    share = bin_count // chan_count
    all_channels = block_width * chan_count
    rounds = plan.shape[0]
    maxlag = (LAGS - 1) // 2
    table = table_on_device(length, bin_count)
    table = (
        table.reshape(length, 2, chan_count, share)
        .transpose(0, 2, 1, 3)
        .reshape(length, 2 * bin_count)
    )
    spec = jnp.dot(samples.reshape(-1, length), table, preferred_element_type=jnp.float32)
    spec = spec.reshape(windows_here, block_width, chan_count, 2, share)
    power = spec[:, :, :, 0] * spec[:, :, :, 0] + spec[:, :, :, 1] * spec[:, :, :, 1]
    level = jnp.mean(power, axis=(2, 3), keepdims=True)
    white = spec / jnp.sqrt(power + 0.1 * level + 1e-06)[:, :, :, None, :]
    white = white.astype(jnp.bfloat16).reshape(windows_here, block_width, 2 * bin_count)
    moved = lax.all_to_all(white, "chan", split_axis=2, concat_axis=1, tiled=True)
    blocks = moved.reshape(windows_here, chan_count, block_width, 2, share)
    mask = valid.astype(jnp.float32)
    weights = jnp.stack([mask * jnp.take(mask, plan[step], axis=1) for step in range(rounds)])
    totals = lax.psum(jnp.sum(weights, axis=1), "tm")
    own = blocks.astype(jnp.float32)
    partial_list = []
    for step in range(rounds):
        other = jnp.take(blocks, plan[step], axis=1).astype(jnp.float32)
        real_part = own[:, :, :, 0] * other[:, :, :, 0] + own[:, :, :, 1] * other[:, :, :, 1]
        imag_part = own[:, :, :, 1] * other[:, :, :, 0] - own[:, :, :, 0] * other[:, :, :, 1]
        product = jnp.stack([real_part, imag_part], axis=3)
        summed = jnp.einsum("wb,wbicf->bicf", weights[step], product)
        summed = summed / totals[step][:, None, None, None]
        partial_list.append(summed.reshape(all_channels, 2 * share))
    partial_value = jnp.stack(partial_list, axis=1)
    lags = lags_on_device(lax.axis_index("chan") * share, share, length, maxlag)
    return lax.psum_scatter(
        jnp.einsum("crk,kl->crl", partial_value, lags, precision=lax.Precision.HIGHEST),
        ("chan", "tm"),
        scatter_dimension=0,
        tiled=True,
    )


def shards(samples, valid, plan):
    chan_count, time_count = lax.axis_size("chan"), lax.axis_size("tm")
    block_width = samples.shape[1]
    rows_each = block_width // (time_count * chan_count)
    whole_tiles = rows_each > 0 and rows_each % STEP == 0 and block_width == rows_each * time_count * chan_count
    whole_tiles = whole_tiles and time_count % (2 * PARTS) == 0 and plan.shape[0] == chan_count - 1
    powers = chan_count & (chan_count - 1) == 0 and chan_count > 1 and time_count % 2 == 0
    if whole_tiles and powers and rows_each * time_count // 2 <= LANES and 2 * plan.shape[0] <= 8:
        return by_channels(samples, valid, plan)
    return by_bins(samples, valid, plan)


def solution(mesh):
    return jax.shard_map(
        shards,
        mesh=mesh,
        in_specs=(P("tm", "chan", None), P("tm", None), P()),
        out_specs=P(("chan", "tm"), None, None),
        check_vma=False,
    )
```
